32 devices in a mesh: grp: 4 (over y, x), en: 8 (over z, core).
Axes of the slice: x: 2, y: 2, z: 4, core: 2. Of those that a mesh axis runs over, the one named last changes fastest.
Arguments:
- lesser: float32 [2, 512, 4096], P(None, 'grp', 'en'), may hold values from -6 to 6
- greater: float32 [2, 512, 4096], P(None, 'grp', 'en'), may hold values from -6 to 6
- mirror: int32 [512], P('grp'), may hold values from 0 to 511, as said below
Outputs:
- polar: float32 [2, 512, 4096], P(None, 'grp', 'en')
The draws below stay inside these ranges and needn't reach their ends.
Inputs may be any that keep to these rules, and one draw needn't show every extreme that they name: mirror is an involution without fixed points; for every entry p, mirror[p] // 16 = (p // 16 + 512 // 32) mod (32), so the mirrored entry lies in the aligned block of 16 entries 512 / 2 entries away.
All inputs are finite; a program needn't handle non-finite values.
Results may differ from the reference program's by a relative error of at most 0.000098.
Values sent between devices are 32-bit elements; how exact they have to be, the bound alone decides.
No kernel may reach another device: no remote copies, remote signals or barrier semaphores. Data moves between devices by JAX's collectives and lax.ppermute only.
A program may use at most 64 MiB of HBM per device.

```python
import jax
import jax.numpy as jnp
from jax import lax

NE = 4096
EN_DEV = 16
NPG = 128
NP = 512
N_GRP = 4


def draw_mirror(key, part):
    blocks = NP // EN_DEV
    half = blocks // 2
    subkeys = jax.random.split(jax.random.fold_in(key, 7), half)
    orders = jax.vmap(lambda sub: jax.random.permutation(sub, EN_DEV))(subkeys).astype(jnp.int32)
    base = jnp.arange(half, dtype=jnp.int32)[:, None] * EN_DEV
    upper = base + half * EN_DEV + orders
    lower = base + jnp.argsort(orders, axis=1, stable=True).astype(jnp.int32)
    return jnp.concatenate([upper.reshape(-1), lower.reshape(-1)]).astype(jnp.int32)


def shard_levels(stream_key, dims, shards, least, high):
    def one(dim, parts):
        heights = jax.random.uniform(jax.random.fold_in(jax.random.fold_in(stream_key, 6), dim), (parts,), jnp.float32, least / len(shards), high / len(shards))
        return jnp.repeat(jnp.exp(heights), dims[dim] // parts).reshape((-1,) + (1,) * (len(dims) - dim - 1))

    factor_of = one(*shards[0])
    for cut in shards[1:]:
        factor_of = factor_of * one(*cut)
    return factor_of


def noise(stream_key, extent, spread, reach, cuts=(), kind=jnp.bfloat16):
    array = spread * jax.random.normal(stream_key, extent, jnp.float32)
    if cuts:
        array = array * shard_levels(stream_key, extent, cuts, -0.22, 0.18)
    return jnp.clip(array, -reach, reach).astype(kind)


def setup_inputs(seed: int = 0) -> dict:
    streams_of = jax.random.split(jax.random.key(seed), 4)
    return {
        "lesser": noise(streams_of[0], (2, NP, NE), 1.0, 6.0, ((1, 4), (2, 8)), jnp.float32),
        "greater": noise(streams_of[1], (2, NP, NE), 1.0, 6.0, ((1, 4), (2, 8)), jnp.float32),
        "mirror": draw_mirror(jax.random.fold_in(streams_of[3], 71), 0),
    }


def reference(lesser, greater, mirror):
    def one_group(start):
        rows_lesser = lax.dynamic_slice_in_dim(lesser, start, NPG, 1)
        partner = lax.dynamic_slice_in_dim(mirror, start, NPG, 0)
        rows_greater = jnp.take(greater, partner, axis=1)
        left = lax.complex(rows_lesser[0], rows_lesser[1])
        right = lax.complex(rows_greater[0], rows_greater[1])
        spectrum = jnp.fft.fft(left, axis=1) * (jnp.fft.ifft(right, axis=1) * NE)
        correl = jnp.fft.ifft(spectrum, axis=1)
        factor = NE ** -0.5
        return jnp.stack([jnp.imag(correl) * factor, -jnp.real(correl) * factor])

    starts = (jnp.arange(N_GRP) * NPG).astype(jnp.int32)
    blocks = lax.map(one_group, starts)
    return jnp.transpose(blocks, (1, 0, 2, 3)).reshape(2, NP, NE)
```

```python
import functools
import math

import jax
import jax.numpy as jnp
import numpy as np
from jax import lax
from jax.experimental import pallas as pl
from jax.experimental.pallas import tpu as pltpu
from jax.sharding import Mesh
from jax.sharding import PartitionSpec as P

LANES = 128
SUBLANES = 8


def dft_block(scale):
    turn = 2.0 * math.pi / LANES * (np.outer(np.arange(LANES), np.arange(LANES)) % LANES)
    cos, sin = np.cos(turn), np.sin(turn)
    full = (np.block([[cos, -sin], [sin, cos]]) * scale).astype(np.float32)
    high = full.astype(jnp.bfloat16)
    low = (full - high.astype(np.float32)).astype(jnp.bfloat16)
    return np.stack([high, low])


def twiddles(points):
    length = points * LANES
    turn = 2.0 * math.pi / length * (np.outer(np.arange(points), np.arange(LANES)) % length)
    return np.stack([np.cos(turn), -np.sin(turn)]).astype(np.float32)


def times_root(value, numerator, denominator):
    re, im = value
    eighths = 8 * numerator / denominator % 8
    if eighths == 0:
        return re, im
    if eighths == 2:
        return im, -re
    if eighths == 4:
        return -re, -im
    if eighths == 6:
        return -im, re
    half = math.sqrt(0.5)
    if eighths == 1:
        return (re + im) * half, (im - re) * half
    if eighths == 3:
        return (im - re) * half, -(re + im) * half
    turn = 2.0 * math.pi * numerator / denominator
    cos, sin = math.cos(turn), math.sin(turn)
    return re * cos + im * sin, im * cos - re * sin


def add(a, b):
    return a[0] + b[0], a[1] + b[1]


def sub(a, b):
    return a[0] - b[0], a[1] - b[1]


def small_dft(values):
    count = len(values)
    if count == 1:
        return values
    even, odd = small_dft(values[0::2]), small_dft(values[1::2])
    odd = [times_root(v, k, count) for k, v in enumerate(odd)]
    return [add(e, o) for e, o in zip(even, odd)] + [sub(e, o) for e, o in zip(even, odd)]


def long_dft(load, keep, points):
    first = min(8, points)
    second = points // first
    for s in range(second):
        for k, value in enumerate(small_dft([load(e * second + s) for e in range(first)])):
            keep[k * second + s, 0], keep[k * second + s, 1] = times_root(value, s * k, points)
    for k in range(first):
        group = [(keep[k * second + s, 0], keep[k * second + s, 1]) for s in range(second)]
        for j, value in enumerate(small_dft(group)):
            yield k + first * j, value


def split_store(ref, row, rows, re, im):
    for place, part in enumerate((re, im)):
        high = part.astype(jnp.bfloat16)
        low = (part - high.astype(jnp.float32)).astype(jnp.bfloat16)
        ref[0, pl.ds(row, rows), place * LANES : (place + 1) * LANES] = high
        ref[1, pl.ds(row, rows), place * LANES : (place + 1) * LANES] = low


def dot(left, right):
    return jnp.dot(left, right, preferred_element_type=jnp.float32)


def lane_dft(halves, table):
    high, low = halves[0], halves[1]
    return dot(high, table[0]) + dot(low, table[0]) + dot(high, table[1])


def pack_kernel(lesser, greater, packed, sems):
    own = lax.axis_index("half")
    copies = []
    count = packed.shape[0] // 2
    rows = packed.shape[2]
    for which, source in enumerate((lesser, greater)):
        place = jnp.where(own == which, 0, count)
        for part in range(2):
            for e in range(count):
                copies.append(
                    pltpu.make_async_copy(
                        source.at[part, pl.ds(e * rows, rows)],
                        packed.at[place + e, part],
                        sems.at[which, part, e],
                    )
                )
    for copy in copies:
        copy.start()
    for copy in copies:
        copy.wait()


def correlate_kernel(mirror, got, forward, backward, twist, out, keep, halves, left, right):
    count = got.shape[0] // 2
    rows = got.shape[2]
    steps = got.shape[3] // LANES
    points = count * steps
    group_rows = mirror.shape[0]
    own = lax.axis_index("half")
    base = lax.axis_index("en") * rows

    def read(start, swap):
        def load(t):
            where = slice(t % steps * LANES, (t % steps + 1) * LANES)
            re = got[start + t // steps, 0, :, where]
            im = got[start + t // steps, 1, :, where]
            return (im, re) if swap else (re, im)

        return load

    def twisted(k, value):
        re, im = value
        cos, sin = twist[0, pl.ds(k, 1), :], twist[1, pl.ds(k, 1), :]
        return re * cos - im * sin, re * sin + im * cos

    for which, target in enumerate((left, right)):
        start = jnp.where(own == which, 0, count)
        for k, value in long_dft(read(start, which == 1), keep, points):
            split_store(halves, k * rows, rows, *twisted(k, value))
        target[...] = lane_dft(halves, forward)

    line = lax.broadcasted_iota(jnp.int32, (rows, LANES), 0)
    order = jnp.zeros((rows, LANES), jnp.int32)
    for row in range(rows):
        order = jnp.where(line == row, mirror[base + row] % group_rows - base, order)
    tiles = rows // SUBLANES
    inner = order % SUBLANES
    tile = order // SUBLANES

    def permuted(value):
        out_tiles = []
        for to in range(tiles):
            span = slice(to * SUBLANES, (to + 1) * SUBLANES)
            result = jnp.zeros((SUBLANES, LANES), jnp.float32)
            for source in range(tiles):
                block = value[source * SUBLANES : (source + 1) * SUBLANES]
                moved = jnp.take_along_axis(block, inner[span], axis=0)
                result = jnp.where(tile[span] == source, moved, result)
            out_tiles.append(result)
        return jnp.concatenate(out_tiles, axis=0)

    for k in range(points):
        span = pl.ds(k * rows, rows)
        a_re, a_im = left[span, :LANES], left[span, LANES:]
        b_im, b_re = permuted(right[span, :LANES]), permuted(right[span, LANES:])
        split_store(halves, k * rows, rows, a_re * b_im + a_im * b_re, a_re * b_re - a_im * b_im)
    left[...] = lane_dft(halves, backward)

    def spectrum(k):
        return twisted(k, (left[pl.ds(k * rows, rows), :LANES], left[pl.ds(k * rows, rows), LANES:]))

    for t, (c_im, c_re) in long_dft(spectrum, keep, points):
        where = slice(t % steps * LANES, (t % steps + 1) * LANES)
        out[t // steps, 0, :, where] = c_im
        out[t // steps, 1, :, where] = -c_re


def body(lesser, greater, mirror):
    _, group_rows, local_len = lesser.shape
    count = lax.axis_size("en")
    rows = group_rows // count
    length = local_len * count
    points = length // LANES
    block = (2, rows, local_len)
    in_vmem = pl.BlockSpec(memory_space=pltpu.VMEM)
    in_place = pl.BlockSpec(memory_space=pl.ANY)

    packed = pl.pallas_call(
        pack_kernel,
        out_shape=jax.ShapeDtypeStruct((2 * count, *block), jnp.float32),
        in_specs=[in_place, in_place],
        out_specs=in_vmem,
        scratch_shapes=[pltpu.SemaphoreType.DMA((2, 2, count))],
        compiler_params=pltpu.CompilerParams(vmem_limit_bytes=8 << 20),
    )(lesser, greater)
    got = lax.all_to_all(packed, ("half", "en"), 0, 0, tiled=True)
    result = pl.pallas_call(
        correlate_kernel,
        out_shape=jax.ShapeDtypeStruct((count, *block), jnp.float32),
        in_specs=[pl.BlockSpec(memory_space=pltpu.SMEM)] + [in_vmem] * 4,
        out_specs=in_vmem,
        scratch_shapes=[
            pltpu.VMEM((points, 2, rows, LANES), jnp.float32),
            pltpu.VMEM((2, points * rows, 2 * LANES), jnp.bfloat16),
            pltpu.VMEM((points * rows, 2 * LANES), jnp.float32),
            pltpu.VMEM((points * rows, 2 * LANES), jnp.float32),
        ],
        compiler_params=pltpu.CompilerParams(vmem_limit_bytes=24 << 20),
    )(
        mirror,
        got,
        jnp.asarray(dft_block(1.0)),
        jnp.asarray(dft_block(length**-1.5)),
        jnp.asarray(twiddles(points)),
    )
    returned = lax.all_to_all(result, "en", 0, 0, tiled=True)
    return jnp.transpose(returned, (1, 0, 2, 3)).reshape(2, group_rows, local_len)


def solution(mesh):
    groups = mesh.shape["grp"]
    devices = mesh.devices.reshape(2, groups // 2, mesh.shape["en"])
    finer = Mesh(devices, ("half", "grp", "en"))
    spec = P(None, ("half", "grp"), "en")
    in_specs = (spec, spec, P(("half", "grp")))
    return jax.shard_map(body, mesh=finer, in_specs=in_specs, out_specs=spec, check_vma=False)
```

```python
import functools
import math

import jax
import jax.numpy as jnp
import numpy as np
from jax import lax
from jax.experimental import pallas as pl
from jax.experimental.pallas import tpu as pltpu
from jax.sharding import Mesh
from jax.sharding import PartitionSpec as P

LANES = 128
SUBLANES = 8


def dft_block(scale):
    turn = 2.0 * math.pi / LANES * (np.outer(np.arange(LANES), np.arange(LANES)) % LANES)
    cos, sin = np.cos(turn), np.sin(turn)
    full = (np.block([[cos, -sin], [sin, cos]]) * scale).astype(np.float32)
    high = full.astype(jnp.bfloat16)
    low = (full - high.astype(np.float32)).astype(jnp.bfloat16)
    return np.stack([high, low])


def twiddles(points):
    length = points * LANES
    turn = 2.0 * math.pi / length * (np.outer(np.arange(points), np.arange(LANES)) % length)
    return np.stack([np.cos(turn), -np.sin(turn)]).astype(np.float32)


def times_root(value, numerator, denominator):
    re, im = value
    eighths = 8 * numerator / denominator % 8
    if eighths == 0:
        return re, im
    if eighths == 2:
        return im, -re
    if eighths == 4:
        return -re, -im
    if eighths == 6:
        return -im, re
    half = math.sqrt(0.5)
    if eighths == 1:
        return (re + im) * half, (im - re) * half
    if eighths == 3:
        return (im - re) * half, -(re + im) * half
    turn = 2.0 * math.pi * numerator / denominator
    cos, sin = math.cos(turn), math.sin(turn)
    return re * cos + im * sin, im * cos - re * sin


def add(a, b):
    return a[0] + b[0], a[1] + b[1]


def sub(a, b):
    return a[0] - b[0], a[1] - b[1]


def small_dft(values):
    count = len(values)
    if count == 1:
        return values
    even, odd = small_dft(values[0::2]), small_dft(values[1::2])
    odd = [times_root(v, k, count) for k, v in enumerate(odd)]
    return [add(e, o) for e, o in zip(even, odd)] + [sub(e, o) for e, o in zip(even, odd)]


def long_dft(load, keep, points):
    first = min(8, points)
    second = points // first
    for s in range(second):
        for k, value in enumerate(small_dft([load(e * second + s) for e in range(first)])):
            keep[k * second + s, 0], keep[k * second + s, 1] = times_root(value, s * k, points)
    for k in range(first):
        group = [(keep[k * second + s, 0], keep[k * second + s, 1]) for s in range(second)]
        for j, value in enumerate(small_dft(group)):
            yield k + first * j, value


def split_store(ref, row, rows, re, im):
    for place, part in enumerate((re, im)):
        high = part.astype(jnp.bfloat16)
        low = (part - high.astype(jnp.float32)).astype(jnp.bfloat16)
        ref[0, pl.ds(row, rows), place * LANES : (place + 1) * LANES] = high
        ref[1, pl.ds(row, rows), place * LANES : (place + 1) * LANES] = low


def dot(left, right):
    return jnp.dot(left, right, preferred_element_type=jnp.float32)


def lane_dft(halves, table):
    high, low = halves[0], halves[1]
    return dot(high, table[0]) + dot(low, table[0]) + dot(high, table[1])


def times_twist(twist, k, value):
    re, im = value
    cos, sin = twist[0, pl.ds(k, 1), :], twist[1, pl.ds(k, 1), :]
    return re * cos - im * sin, re * sin + im * cos


def pack_kernel(mirror, lesser, greater, packed, *rest):
    blocks, (held, block_sems, chunk_sems, held_sems) = rest[:-4], rest[-4:]
    _, count, tiles, sub, local_len = lesser.shape
    rows = tiles * sub
    own = lax.axis_index("half")
    me = lax.axis_index("en")
    loads = [pltpu.make_async_copy(greater.at[p], held.at[p], held_sems.at[p]) for p in range(2)]
    moves = [
        pltpu.make_async_copy(
            lesser.at[p, :, 0], packed.at[pl.ds(own * count, count), p], chunk_sems.at[p]
        )
        for p in range(2)
    ]
    moves += [
        pltpu.make_async_copy(lesser.at[:, me ^ s, 1], blocks[s], block_sems.at[s])
        for s in range(count)
    ]
    for copy in loads + moves:
        copy.start()
    line = lax.broadcasted_iota(jnp.int32, (sub, LANES), 0)
    for copy in loads:
        copy.wait()
    for s in range(count):
        to = me ^ s
        orders = [jnp.zeros((sub, LANES), jnp.int32) for _ in range(tiles)]
        for row in range(rows):
            place = mirror[to * rows + row] % rows
            orders = [jnp.where(line + t * sub == place, row, o) for t, o in enumerate(orders)]
        for part in range(2):
            for lane in range(0, local_len, LANES):
                span = slice(lane, lane + LANES)
                sources = [held[part, to, t, :, span] for t in range(tiles)]
                for t, order in enumerate(orders):
                    moved = jnp.zeros((sub, LANES), jnp.float32)
                    for u, source in enumerate(sources):
                        picked = jnp.take_along_axis(source, order % sub, axis=0)
                        moved = jnp.where(order // sub == u, picked, moved)
                    if t == 0:
                        packed[(1 - own) * count + to, part, :, span] = moved
                    else:
                        blocks[count + s][part, :, span] = moved
    for copy in moves:
        copy.wait()


def correlate(got, forward, backward, twist, out, keep, halves, left, right):
    count = got.shape[0] // 2
    rows = got.shape[2]
    steps = got.shape[3] // LANES
    points = count * steps
    own = lax.axis_index("half")

    def read(start, swap):
        def load(t):
            where = slice(t % steps * LANES, (t % steps + 1) * LANES)
            re = got[start + t // steps, 0, :, where]
            im = got[start + t // steps, 1, :, where]
            return (im, re) if swap else (re, im)

        return load

    for which, target in enumerate((left, right)):
        start = jnp.where(own == which, 0, count)
        for k, value in long_dft(read(start, which == 1), keep, points):
            split_store(halves, k * rows, rows, *times_twist(twist, k, value))
        target[...] = lane_dft(halves, forward)

    for k in range(points):
        span = pl.ds(k * rows, rows)
        a_re, a_im = left[span, :LANES], left[span, LANES:]
        b_im, b_re = right[span, :LANES], right[span, LANES:]
        split_store(halves, k * rows, rows, a_re * b_im + a_im * b_re, a_re * b_re - a_im * b_im)
    left[...] = lane_dft(halves, backward)

    def spectrum(k):
        span = pl.ds(k * rows, rows)
        return times_twist(twist, k, (left[span, :LANES], left[span, LANES:]))

    for t, (c_im, c_re) in long_dft(spectrum, keep, points):
        where = slice(t % steps * LANES, (t % steps + 1) * LANES)
        out[t // steps, 0, :, where] = c_im
        out[t // steps, 1, :, where] = -c_re


def correlate_pieces(pieces, *refs):
    got, blocks, rest = refs[-1], refs[:pieces], refs[pieces:-1]
    count = pieces // 2
    own = lax.axis_index("half")
    me = lax.axis_index("en")
    for s, block in enumerate(blocks):
        half = own if s < count else 1 - own
        got[half * count + (me ^ (s % count))] = block[...]
    correlate(got, *rest)


def hold_kernel(block, out):
    out[...] = block[...]


def far_first(count):
    return sorted(range(1, 2 * count), key=lambda s: (-(s % count // 2), s < count, s))


def unpack_kernel(chunk, *refs):
    returned, out, sems = refs[0], refs[-2], refs[-1]
    copies = [
        pltpu.make_async_copy(returned.at[:, p], out.at[p, :, chunk], sems.at[p]) for p in range(2)
    ]
    for copy in copies:
        copy.start()
    for copy in copies:
        copy.wait()


def body(lesser, greater, mirror):
    _, group_rows, local_len = lesser.shape
    count = lax.axis_size("en")
    rows = group_rows // count
    tiles = rows // SUBLANES
    length = local_len * count
    points = length // LANES
    block = (2, SUBLANES, local_len)
    tiled = (2, count, tiles, SUBLANES, local_len)
    f32 = jnp.float32
    in_vmem = pl.BlockSpec(memory_space=pltpu.VMEM)
    in_smem = pl.BlockSpec(memory_space=pltpu.SMEM)
    in_hbm = pl.BlockSpec(memory_space=pltpu.HBM)
    pieces = 2 * count

    packed, *blocks = pl.pallas_call(
        pack_kernel,
        out_shape=[jax.ShapeDtypeStruct((pieces, *block), f32)]
        + [jax.ShapeDtypeStruct(block, f32)] * pieces,
        in_specs=[in_smem, in_hbm, in_hbm],
        out_specs=[in_vmem] * (1 + pieces),
        scratch_shapes=[
            pltpu.VMEM(tiled, f32),
            pltpu.SemaphoreType.DMA((count,)),
            pltpu.SemaphoreType.DMA((2,)),
            pltpu.SemaphoreType.DMA((2,)),
        ],
        compiler_params=pltpu.CompilerParams(vmem_limit_bytes=8 << 20),
        cost_estimate=pl.CostEstimate(flops=1 << 20, bytes_accessed=4 << 20, transcendentals=0),
    )(mirror, *(pltpu.with_memory_space_constraint(x.reshape(tiled), pltpu.HBM) for x in (lesser, greater)))

    got = lax.all_to_all(packed, ("half", "en"), 0, 0, tiled=True)
    arrived = list(blocks)
    arrived[0] = pl.pallas_call(
        hold_kernel,
        out_shape=jax.ShapeDtypeStruct(block, f32),
        in_specs=[in_vmem],
        out_specs=in_vmem,
        compiler_params=pltpu.CompilerParams(vmem_limit_bytes=1 << 20),
    )(blocks[0])
    for s in far_first(count):
        route = [(d, d ^ s) for d in range(pieces)]
        arrived[s] = lax.ppermute(blocks[s], ("half", "en"), route)

    tables = (
        jnp.asarray(dft_block(1.0)),
        jnp.asarray(dft_block(length**-1.5)),
        jnp.asarray(twiddles(points)),
    )
    settings = dict(
        out_shape=jax.ShapeDtypeStruct((count, *block), f32),
        out_specs=in_vmem,
        compiler_params=pltpu.CompilerParams(vmem_limit_bytes=16 << 20),
        cost_estimate=pl.CostEstimate(
            flops=3 * 2 * 3 * points * SUBLANES * 4 * LANES * LANES,
            bytes_accessed=4 << 20,
            transcendentals=0,
        ),
    )
    scratch = [
        pltpu.VMEM((points, 2, SUBLANES, LANES), f32),
        pltpu.VMEM((2, points * SUBLANES, 2 * LANES), jnp.bfloat16),
        pltpu.VMEM((points * SUBLANES, 2 * LANES), f32),
        pltpu.VMEM((points * SUBLANES, 2 * LANES), f32),
    ]
    result_a = pl.pallas_call(
        correlate, in_specs=[in_vmem] * 4, scratch_shapes=scratch, **settings
    )(got, *tables)
    back_a = lax.all_to_all(result_a, "en", 0, 0, tiled=True)
    result_b = pl.pallas_call(
        functools.partial(correlate_pieces, pieces),
        in_specs=[in_vmem] * (pieces + 3),
        scratch_shapes=scratch + [pltpu.VMEM((pieces, *block), f32)],
        **settings,
    )(*arrived, *tables)
    back_b = lax.all_to_all(result_b, "en", 0, 0, tiled=True)

    def unpack(chunk, returned, *held):
        return pl.pallas_call(
            functools.partial(unpack_kernel, chunk),
            out_shape=jax.ShapeDtypeStruct(tiled, f32),
            in_specs=[in_vmem] + [in_hbm] * len(held),
            out_specs=in_hbm,
            scratch_shapes=[pltpu.SemaphoreType.DMA((2,))],
            input_output_aliases={1: 0} if held else {},
            compiler_params=pltpu.CompilerParams(vmem_limit_bytes=1 << 20),
        )(returned, *held)

    kept = unpack(0, back_a)
    out = unpack(1, back_b, kept)
    return out.reshape(2, group_rows, local_len)


def solution(mesh):
    groups = mesh.shape["grp"]
    devices = mesh.devices.reshape(2, groups // 2, mesh.shape["en"])
    finer = Mesh(devices, ("half", "grp", "en"))
    spec = P(None, ("half", "grp"), "en")
    in_specs = (spec, spec, P(("half", "grp")))

    return jax.shard_map(body, mesh=finer, in_specs=in_specs, out_specs=spec, check_vma=False)
```

```python
import functools
import math

import jax
import jax.numpy as jnp
import numpy as np
from jax import lax
from jax.experimental import pallas as pl
from jax.experimental.pallas import tpu as pltpu
from jax.sharding import Mesh
from jax.sharding import PartitionSpec as P

LANES = 128
SUBLANES = 8


def dft_block(scale):
    turn = 2.0 * math.pi / LANES * (np.outer(np.arange(LANES), np.arange(LANES)) % LANES)
    cos, sin = np.cos(turn), np.sin(turn)
    full = (np.block([[cos, -sin], [sin, cos]]) * scale).astype(np.float32)
    high = full.astype(jnp.bfloat16)
    low = (full - high.astype(np.float32)).astype(jnp.bfloat16)
    return np.stack([high, low])


def twiddles(points):
    length = points * LANES
    turn = 2.0 * math.pi / length * (np.outer(np.arange(points), np.arange(LANES)) % length)
    return np.stack([np.cos(turn), -np.sin(turn)]).astype(np.float32)


def times_root(value, numerator, denominator):
    re, im = value
    eighths = 8 * numerator / denominator % 8
    if eighths == 0:
        return re, im
    if eighths == 2:
        return im, -re
    if eighths == 4:
        return -re, -im
    if eighths == 6:
        return -im, re
    half = math.sqrt(0.5)
    if eighths == 1:
        return (re + im) * half, (im - re) * half
    if eighths == 3:
        return (im - re) * half, -(re + im) * half
    turn = 2.0 * math.pi * numerator / denominator
    cos, sin = math.cos(turn), math.sin(turn)
    return re * cos + im * sin, im * cos - re * sin


def add(a, b):
    return a[0] + b[0], a[1] + b[1]


def sub(a, b):
    return a[0] - b[0], a[1] - b[1]


def small_dft(values):
    count = len(values)
    if count == 1:
        return values
    even, odd = small_dft(values[0::2]), small_dft(values[1::2])
    odd = [times_root(v, k, count) for k, v in enumerate(odd)]
    return [add(e, o) for e, o in zip(even, odd)] + [sub(e, o) for e, o in zip(even, odd)]


def long_dft(load, keep, points):
    first = min(8, points)
    second = points // first
    for s in range(second):
        for k, value in enumerate(small_dft([load(e * second + s) for e in range(first)])):
            keep[k * second + s, 0], keep[k * second + s, 1] = times_root(value, s * k, points)
    for k in range(first):
        group = [(keep[k * second + s, 0], keep[k * second + s, 1]) for s in range(second)]
        for j, value in enumerate(small_dft(group)):
            yield k + first * j, value


def split_store(ref, row, rows, re, im):
    for place, part in enumerate((re, im)):
        high = part.astype(jnp.bfloat16)
        low = (part - high.astype(jnp.float32)).astype(jnp.bfloat16)
        ref[0, pl.ds(row, rows), place * LANES : (place + 1) * LANES] = high
        ref[1, pl.ds(row, rows), place * LANES : (place + 1) * LANES] = low


def dot(left, right):
    return jnp.dot(left, right, preferred_element_type=jnp.float32)


def lane_dft(halves, table):
    high, low = halves[0], halves[1]
    return dot(high, table[0]) + dot(low, table[0]) + dot(high, table[1])


def times_twist(twist, k, value):
    re, im = value
    cos, sin = twist[0, pl.ds(k, 1), :], twist[1, pl.ds(k, 1), :]
    return re * cos - im * sin, re * sin + im * cos


def pack_kernel(mirror, lesser, greater, packed, second, places, held, ready, sems):
    _, count, tiles, sub, local_len = lesser.shape
    rows = tiles * sub
    own = lax.axis_index("half")
    loads = [pltpu.make_async_copy(mirror, places, sems.at[0])]
    loads += [pltpu.make_async_copy(greater.at[p], held.at[p], sems.at[1 + p]) for p in range(2)]
    firsts = [
        pltpu.make_async_copy(lesser.at[p, :, 0], ready.at[0, :, p], sems.at[3 + p])
        for p in range(2)
    ]
    for copy in loads + firsts:
        copy.start()
    stores = [
        pltpu.make_async_copy(ready.at[0], packed.at[pl.ds(own * count, count)], sems.at[5]),
        pltpu.make_async_copy(ready.at[1], packed.at[pl.ds((1 - own) * count, count)], sems.at[6]),
    ]
    loads[0].wait()
    lane = lax.broadcasted_iota(jnp.int32, (rows, count * rows), 1)
    line = lax.broadcasted_iota(jnp.int32, (rows, count * rows), 0)
    goal = jnp.broadcast_to(places[...], (rows, count * rows)) % rows
    source = jnp.where(goal == line, (lane % rows).astype(jnp.float32), 0.0)
    orders = [
        jnp.sum(jnp.where(lane // rows == to, source, 0.0), axis=1, keepdims=True).astype(jnp.int32)
        for to in range(count)
    ]
    for copy in firsts:
        copy.wait()
    stores[0].start()
    for part in range(2):
        loads[1 + part].wait()
        for to in range(count):
            order = jnp.broadcast_to(orders[to], (rows, LANES))
            for start in range(0, local_len, LANES):
                span = slice(start, start + LANES)
                tiles_in = [held[part, to, u, :, span] for u in range(tiles)]
                for t in range(tiles):
                    wanted = order[t * sub : (t + 1) * sub]
                    moved = jnp.zeros((sub, LANES), jnp.float32)
                    for u, tile in enumerate(tiles_in):
                        picked = jnp.take_along_axis(tile, wanted % sub, axis=0)
                        moved = jnp.where(wanted // sub == u, picked, moved)
                    if t == 0:
                        ready[1, to, part, :, span] = moved
                    else:
                        second[to, part, :, span] = moved
    stores[1].start()
    for copy in stores:
        copy.wait()


def split_kernel(lesser, second, mine, give, sems):
    chips = mine.shape[1]
    me = lax.axis_index("en")
    copies = []
    for z in range(chips):
        for core, target in enumerate((mine, give)):
            to = me ^ (2 * z + core)
            copies.append(
                pltpu.make_async_copy(lesser.at[:, to, 1], target.at[0, z], sems.at[core, z])
            )
    for copy in copies:
        copy.start()
    for z in range(chips):
        for core, target in enumerate((mine, give)):
            target[1, z] = second[me ^ (2 * z + core)]
    for copy in copies:
        copy.wait()


def join_kernel(mine, got, *outs):
    chips = mine.shape[1]
    for t, out in enumerate(outs):
        out[0] = mine[t // chips, t % chips]
        out[1] = got[t // chips, t % chips]


def correlate(got, forward, backward, twist, out, keep, halves, left, right):
    count = got.shape[0] // 2
    rows = got.shape[2]
    steps = got.shape[3] // LANES
    points = count * steps
    own = lax.axis_index("half")

    def read(start, swap):
        def load(t):
            where = slice(t % steps * LANES, (t % steps + 1) * LANES)
            re = got[start + t // steps, 0, :, where]
            im = got[start + t // steps, 1, :, where]
            return (im, re) if swap else (re, im)

        return load

    for which, target in enumerate((left, right)):
        start = jnp.where(own == which, 0, count)
        for k, value in long_dft(read(start, which == 1), keep, points):
            split_store(halves, k * rows, rows, *times_twist(twist, k, value))
        target[...] = lane_dft(halves, forward)

    for k in range(points):
        span = pl.ds(k * rows, rows)
        a_re, a_im = left[span, :LANES], left[span, LANES:]
        b_im, b_re = right[span, :LANES], right[span, LANES:]
        split_store(halves, k * rows, rows, a_re * b_im + a_im * b_re, a_re * b_re - a_im * b_im)
    left[...] = lane_dft(halves, backward)

    def spectrum(k):
        span = pl.ds(k * rows, rows)
        return times_twist(twist, k, (left[span, :LANES], left[span, LANES:]))

    for t, (c_im, c_re) in long_dft(spectrum, keep, points):
        where = slice(t % steps * LANES, (t % steps + 1) * LANES)
        out[t // steps, 0, :, where] = c_im
        out[t // steps, 1, :, where] = -c_re


def correlate_pieces(pieces, *refs):
    got, blocks, rest = refs[-1], refs[:pieces], refs[pieces:-1]
    chips = pieces // 2
    own = lax.axis_index("half")
    me = lax.axis_index("en")
    for t, block in enumerate(blocks):
        half = own if t < chips else 1 - own
        for core in range(2):
            got[half * (2 * chips) + (me ^ (2 * (t % chips) + core))] = block[core]
    correlate(got, *rest)


def hold_kernel(block, out):
    out[...] = block[...]


def far_first(chips):
    return sorted(range(1, 2 * chips), key=lambda t: (-(t % chips), t < chips))


def unpack_kernel(chunk, *refs):
    returned, out, sems = refs[0], refs[-2], refs[-1]
    copies = [
        pltpu.make_async_copy(returned.at[:, p], out.at[p, :, chunk], sems.at[p]) for p in range(2)
    ]
    for copy in copies:
        copy.start()
    for copy in copies:
        copy.wait()


def body(lesser, greater, mirror):
    _, group_rows, local_len = lesser.shape
    count = lax.axis_size("en")
    rows = group_rows // count
    tiles = rows // SUBLANES
    length = local_len * count
    points = length // LANES
    block = (2, SUBLANES, local_len)
    tiled = (2, count, tiles, SUBLANES, local_len)
    f32 = jnp.float32
    in_vmem = pl.BlockSpec(memory_space=pltpu.VMEM)
    in_smem = pl.BlockSpec(memory_space=pltpu.SMEM)
    in_hbm = pl.BlockSpec(memory_space=pltpu.HBM)

    chips = count // 2
    half_view = (2, chips, *block)
    bundle = jax.ShapeDtypeStruct((2, *block), f32)
    mirror, lesser, greater = (
        pltpu.with_memory_space_constraint(x, pltpu.HBM)
        for x in (mirror[None], lesser.reshape(tiled), greater.reshape(tiled))
    )
    packed, second = pl.pallas_call(
        pack_kernel,
        out_shape=[
            jax.ShapeDtypeStruct((2 * count, *block), f32),
            jax.ShapeDtypeStruct((count, *block), f32),
        ],
        in_specs=[in_hbm] * 3,
        out_specs=[in_hbm, in_vmem],
        scratch_shapes=[
            pltpu.VMEM((1, group_rows), jnp.int32),
            pltpu.VMEM(tiled, f32),
            pltpu.VMEM((2, count, *block), f32),
            pltpu.SemaphoreType.DMA((7,)),
        ],
        compiler_params=pltpu.CompilerParams(vmem_limit_bytes=8 << 20),
    )(mirror, lesser, greater)
    got = lax.all_to_all(packed, ("half", "en"), 0, 0, tiled=True)
    mine, give = pl.pallas_call(
        split_kernel,
        out_shape=[jax.ShapeDtypeStruct(half_view, f32)] * 2,
        in_specs=[in_hbm, in_vmem],
        out_specs=[in_vmem] * 2,
        scratch_shapes=[pltpu.SemaphoreType.DMA((2, chips))],
        compiler_params=pltpu.CompilerParams(vmem_limit_bytes=4 << 20),
    )(lesser, second)
    given = lax.ppermute(give, "en", [(e, e ^ 1) for e in range(count)])
    bundles = pl.pallas_call(
        join_kernel,
        out_shape=[bundle] * (2 * chips),
        in_specs=[in_vmem] * 2,
        out_specs=[in_vmem] * (2 * chips),
        compiler_params=pltpu.CompilerParams(vmem_limit_bytes=4 << 20),
    )(mine, given)
    arrived = list(bundles)
    arrived[0] = pl.pallas_call(
        hold_kernel,
        out_shape=bundle,
        in_specs=[in_vmem],
        out_specs=in_vmem,
        compiler_params=pltpu.CompilerParams(vmem_limit_bytes=1 << 20),
    )(bundles[0])
    for t in far_first(chips):
        step = t // chips * count + 2 * (t % chips)
        route = [(d, d ^ step) for d in range(2 * count)]
        arrived[t] = lax.ppermute(bundles[t], ("half", "en"), route)

    tables = (
        jnp.asarray(dft_block(1.0)),
        jnp.asarray(dft_block(length**-1.5)),
        jnp.asarray(twiddles(points)),
    )
    settings = dict(
        out_shape=jax.ShapeDtypeStruct((count, *block), f32),
        out_specs=in_vmem,
        compiler_params=pltpu.CompilerParams(vmem_limit_bytes=16 << 20),
        cost_estimate=pl.CostEstimate(
            flops=3 * 2 * 3 * points * SUBLANES * 4 * LANES * LANES,
            bytes_accessed=4 << 20,
            transcendentals=0,
        ),
    )
    scratch = [
        pltpu.VMEM((points, 2, SUBLANES, LANES), f32),
        pltpu.VMEM((2, points * SUBLANES, 2 * LANES), jnp.bfloat16),
        pltpu.VMEM((points * SUBLANES, 2 * LANES), f32),
        pltpu.VMEM((points * SUBLANES, 2 * LANES), f32),
    ]
    result_a = pl.pallas_call(
        correlate, in_specs=[in_vmem] * 4, scratch_shapes=scratch, **settings
    )(got, *tables)
    back_a = lax.all_to_all(result_a, "en", 0, 0, tiled=True)
    result_b = pl.pallas_call(
        functools.partial(correlate_pieces, 2 * chips),
        in_specs=[in_vmem] * (2 * chips + 3),
        scratch_shapes=scratch + [pltpu.VMEM((2 * count, *block), f32)],
        **settings,
    )(*arrived, *tables)
    back_b = lax.all_to_all(result_b, "en", 0, 0, tiled=True)

    def unpack(chunk, returned, *held):
        return pl.pallas_call(
            functools.partial(unpack_kernel, chunk),
            out_shape=jax.ShapeDtypeStruct(tiled, f32),
            in_specs=[in_vmem] + [in_hbm] * len(held),
            out_specs=in_hbm,
            scratch_shapes=[pltpu.SemaphoreType.DMA((2,))],
            input_output_aliases={1: 0} if held else {},
            compiler_params=pltpu.CompilerParams(vmem_limit_bytes=1 << 20),
        )(returned, *held)

    kept = unpack(0, back_a)
    out = unpack(1, back_b, kept)
    return out.reshape(2, group_rows, local_len)


def solution(mesh):
    groups = mesh.shape["grp"]
    devices = mesh.devices.reshape(2, groups // 2, mesh.shape["en"])
    finer = Mesh(devices, ("half", "grp", "en"))
    spec = P(None, ("half", "grp"), "en")
    in_specs = (spec, spec, P(("half", "grp")))

    return jax.shard_map(body, mesh=finer, in_specs=in_specs, out_specs=spec, check_vma=False)
```

```python
import functools
import math

import jax
import jax.numpy as jnp
import numpy as np
from jax import lax
from jax.experimental import pallas as pl
from jax.experimental.pallas import tpu as pltpu
from jax.sharding import Mesh
from jax.sharding import PartitionSpec as P

LANES = 128
SUBLANES = 8


def dft_block(scale):
    turn = 2.0 * math.pi / LANES * (np.outer(np.arange(LANES), np.arange(LANES)) % LANES)
    cos, sin = np.cos(turn), np.sin(turn)
    full = (np.block([[cos, -sin], [sin, cos]]) * scale).astype(np.float32)
    high = full.astype(jnp.bfloat16)
    low = (full - high.astype(np.float32)).astype(jnp.bfloat16)
    return np.stack([high, low])


def twiddles(points):
    length = points * LANES
    turn = 2.0 * math.pi / length * (np.outer(np.arange(points), np.arange(LANES)) % length)
    return np.stack([np.cos(turn), -np.sin(turn)]).astype(np.float32)


def times_root(value, numerator, denominator):
    re, im = value
    eighths = 8 * numerator / denominator % 8
    if eighths == 0:
        return re, im
    if eighths == 2:
        return im, -re
    if eighths == 4:
        return -re, -im
    if eighths == 6:
        return -im, re
    half = math.sqrt(0.5)
    if eighths == 1:
        return (re + im) * half, (im - re) * half
    if eighths == 3:
        return (im - re) * half, -(re + im) * half
    turn = 2.0 * math.pi * numerator / denominator
    cos, sin = math.cos(turn), math.sin(turn)
    return re * cos + im * sin, im * cos - re * sin


def add(a, b):
    return a[0] + b[0], a[1] + b[1]


def sub(a, b):
    return a[0] - b[0], a[1] - b[1]


def small_dft(values):
    count = len(values)
    if count == 1:
        return values
    even, odd = small_dft(values[0::2]), small_dft(values[1::2])
    odd = [times_root(v, k, count) for k, v in enumerate(odd)]
    return [add(e, o) for e, o in zip(even, odd)] + [sub(e, o) for e, o in zip(even, odd)]


def long_dft(load, keep, points):
    first = min(8, points)
    second = points // first
    for s in range(second):
        for k, value in enumerate(small_dft([load(e * second + s) for e in range(first)])):
            keep[k * second + s, 0], keep[k * second + s, 1] = times_root(value, s * k, points)
    for k in range(first):
        group = [(keep[k * second + s, 0], keep[k * second + s, 1]) for s in range(second)]
        for j, value in enumerate(small_dft(group)):
            yield k + first * j, value


def split_store(ref, row, rows, re, im):
    for place, part in enumerate((re, im)):
        high = part.astype(jnp.bfloat16)
        low = (part - high.astype(jnp.float32)).astype(jnp.bfloat16)
        ref[0, pl.ds(row, rows), place * LANES : (place + 1) * LANES] = high
        ref[1, pl.ds(row, rows), place * LANES : (place + 1) * LANES] = low


def dot(left, right):
    return jnp.dot(left, right, preferred_element_type=jnp.float32)


def lane_dft(halves, table):
    high, low = halves[0], halves[1]
    return dot(high, table[0]) + dot(low, table[0]) + dot(high, table[1])


def times_twist(twist, k, value):
    re, im = value
    cos, sin = twist[0, pl.ds(k, 1), :], twist[1, pl.ds(k, 1), :]
    return re * cos - im * sin, re * sin + im * cos


def pack_kernel(mirror, lesser, greater, packed, second, places, held, ready, sems):
    _, count, tiles, sub, local_len = lesser.shape
    rows = tiles * sub
    own = lax.axis_index("half")
    loads = [pltpu.make_async_copy(mirror, places, sems.at[0])]
    loads += [pltpu.make_async_copy(greater.at[p], held.at[p], sems.at[1 + p]) for p in range(2)]
    firsts = [
        pltpu.make_async_copy(lesser.at[p, :, 0], ready.at[0, :, p], sems.at[3 + p])
        for p in range(2)
    ]
    for copy in loads + firsts:
        copy.start()
    stores = [
        pltpu.make_async_copy(ready.at[0], packed.at[pl.ds(own * count, count)], sems.at[5]),
        pltpu.make_async_copy(ready.at[1], packed.at[pl.ds((1 - own) * count, count)], sems.at[6]),
    ]
    loads[0].wait()
    lane = lax.broadcasted_iota(jnp.int32, (rows, count * rows), 1)
    line = lax.broadcasted_iota(jnp.int32, (rows, count * rows), 0)
    goal = jnp.broadcast_to(places[...], (rows, count * rows)) % rows
    source = jnp.where(goal == line, (lane % rows).astype(jnp.float32), 0.0)
    orders = [
        jnp.sum(jnp.where(lane // rows == to, source, 0.0), axis=1, keepdims=True).astype(jnp.int32)
        for to in range(count)
    ]
    for copy in firsts:
        copy.wait()
    stores[0].start()
    for part in range(2):
        loads[1 + part].wait()
        for to in range(count):
            order = jnp.broadcast_to(orders[to], (rows, LANES))
            for start in range(0, local_len, LANES):
                span = slice(start, start + LANES)
                tiles_in = [held[part, to, u, :, span] for u in range(tiles)]
                for t in range(tiles):
                    wanted = order[t * sub : (t + 1) * sub]
                    moved = jnp.zeros((sub, LANES), jnp.float32)
                    for u, tile in enumerate(tiles_in):
                        picked = jnp.take_along_axis(tile, wanted % sub, axis=0)
                        moved = jnp.where(wanted // sub == u, picked, moved)
                    if t == 0:
                        ready[1, to, part, :, span] = moved
                    else:
                        second[to, part, :, span] = moved
    stores[1].start()
    for copy in stores:
        copy.wait()


def split_kernel(lesser, second, mine, give, sems):
    chips = mine.shape[1]
    me = lax.axis_index("en")
    copies = []
    for z in range(chips):
        for core, target in enumerate((mine, give)):
            to = me ^ (2 * z + core)
            copies.append(
                pltpu.make_async_copy(lesser.at[:, to, 1], target.at[0, z], sems.at[core, z])
            )
    for copy in copies:
        copy.start()
    for z in range(chips):
        for core, target in enumerate((mine, give)):
            target[1, z] = second[me ^ (2 * z + core)]
    for copy in copies:
        copy.wait()


def join_kernel(mine, got, *outs):
    chips = mine.shape[1]
    for t, out in enumerate(outs):
        out[0] = mine[t // chips, t % chips]
        out[1] = got[t // chips, t % chips]


def join_back_kernel(mine, got, *outs):
    for z, out in enumerate(outs):
        out[0] = mine[z]
        out[1] = got[z]


def correlate(got, forward, backward, twist, out, keep, halves, left, right):
    count = got.shape[0] // 2
    rows = got.shape[2]
    steps = got.shape[3] // LANES
    points = count * steps
    own = lax.axis_index("half")

    def read(start, swap):
        def load(t):
            where = slice(t % steps * LANES, (t % steps + 1) * LANES)
            re = got[start + t // steps, 0, :, where]
            im = got[start + t // steps, 1, :, where]
            return (im, re) if swap else (re, im)

        return load

    for which, target in enumerate((left, right)):
        start = jnp.where(own == which, 0, count)
        for k, value in long_dft(read(start, which == 1), keep, points):
            split_store(halves, k * rows, rows, *times_twist(twist, k, value))
        target[...] = lane_dft(halves, forward)

    for k in range(points):
        span = pl.ds(k * rows, rows)
        a_re, a_im = left[span, :LANES], left[span, LANES:]
        b_im, b_re = right[span, :LANES], right[span, LANES:]
        split_store(halves, k * rows, rows, a_re * b_im + a_im * b_re, a_re * b_re - a_im * b_im)
    left[...] = lane_dft(halves, backward)

    def spectrum(k):
        span = pl.ds(k * rows, rows)
        return times_twist(twist, k, (left[span, :LANES], left[span, LANES:]))

    for t, (c_im, c_re) in long_dft(spectrum, keep, points):
        where = slice(t % steps * LANES, (t % steps + 1) * LANES)
        out[t // steps, 0, :, where] = c_im
        out[t // steps, 1, :, where] = -c_re


def correlate_pieces(pieces, *refs):
    blocks, (forward, backward, twist, mine, give) = refs[:pieces], refs[pieces : pieces + 5]
    got, out, *rest = refs[pieces + 5 :]
    chips = pieces // 2
    own = lax.axis_index("half")
    me = lax.axis_index("en")
    for t, block in enumerate(blocks):
        half = own if t < chips else 1 - own
        for core in range(2):
            got[half * (2 * chips) + (me ^ (2 * (t % chips) + core))] = block[core]
    correlate(got, forward, backward, twist, out, *rest)
    for z in range(chips):
        for core, target in enumerate((mine, give)):
            target[z] = out[me ^ (2 * z + core)]


def hold_kernel(block, out):
    out[...] = block[...]


def far_first(chips):
    return sorted(range(1, 2 * chips), key=lambda t: (-(t % chips), t < chips))


def keep_first_kernel(returned, out, sems):
    copies = [
        pltpu.make_async_copy(returned.at[:, p], out.at[p, :, 0], sems.at[p]) for p in range(2)
    ]
    for copy in copies:
        copy.start()
    for copy in copies:
        copy.wait()


def keep_second_kernel(*refs):
    *bundles, _, out, sems = refs
    me = lax.axis_index("en")
    copies = [
        pltpu.make_async_copy(
            bundle.at[core], out.at[:, me ^ (2 * z + core), 1], sems.at[z, core]
        )
        for z, bundle in enumerate(bundles)
        for core in range(2)
    ]
    for copy in copies:
        copy.start()
    for copy in copies:
        copy.wait()


def body(lesser, greater, mirror):
    _, group_rows, local_len = lesser.shape
    count = lax.axis_size("en")
    rows = group_rows // count
    tiles = rows // SUBLANES
    length = local_len * count
    points = length // LANES
    block = (2, SUBLANES, local_len)
    tiled = (2, count, tiles, SUBLANES, local_len)
    f32 = jnp.float32
    in_vmem = pl.BlockSpec(memory_space=pltpu.VMEM)
    in_smem = pl.BlockSpec(memory_space=pltpu.SMEM)
    in_hbm = pl.BlockSpec(memory_space=pltpu.HBM)

    chips = count // 2
    half_view = (2, chips, *block)
    bundle = jax.ShapeDtypeStruct((2, *block), f32)
    mirror, lesser, greater = (
        pltpu.with_memory_space_constraint(x, pltpu.HBM)
        for x in (mirror[None], lesser.reshape(tiled), greater.reshape(tiled))
    )
    packed, second = pl.pallas_call(
        pack_kernel,
        out_shape=[
            jax.ShapeDtypeStruct((2 * count, *block), f32),
            jax.ShapeDtypeStruct((count, *block), f32),
        ],
        in_specs=[in_hbm] * 3,
        out_specs=[in_hbm, in_vmem],
        scratch_shapes=[
            pltpu.VMEM((1, group_rows), jnp.int32),
            pltpu.VMEM(tiled, f32),
            pltpu.VMEM((2, count, *block), f32),
            pltpu.SemaphoreType.DMA((7,)),
        ],
        compiler_params=pltpu.CompilerParams(vmem_limit_bytes=8 << 20),
    )(mirror, lesser, greater)
    got = lax.all_to_all(packed, ("half", "en"), 0, 0, tiled=True)
    mine, give = pl.pallas_call(
        split_kernel,
        out_shape=[jax.ShapeDtypeStruct(half_view, f32)] * 2,
        in_specs=[in_hbm, in_vmem],
        out_specs=[in_vmem] * 2,
        scratch_shapes=[pltpu.SemaphoreType.DMA((2, chips))],
        compiler_params=pltpu.CompilerParams(vmem_limit_bytes=4 << 20),
    )(lesser, second)
    given = lax.ppermute(give, "en", [(e, e ^ 1) for e in range(count)])
    bundles = pl.pallas_call(
        join_kernel,
        out_shape=[bundle] * (2 * chips),
        in_specs=[in_vmem] * 2,
        out_specs=[in_vmem] * (2 * chips),
        compiler_params=pltpu.CompilerParams(vmem_limit_bytes=4 << 20),
    )(mine, given)
    arrived = list(bundles)
    arrived[0] = pl.pallas_call(
        hold_kernel,
        out_shape=bundle,
        in_specs=[in_vmem],
        out_specs=in_vmem,
        compiler_params=pltpu.CompilerParams(vmem_limit_bytes=1 << 20),
    )(bundles[0])
    for t in far_first(chips):
        step = t // chips * count + 2 * (t % chips)
        route = [(d, d ^ step) for d in range(2 * count)]
        arrived[t] = lax.ppermute(bundles[t], ("half", "en"), route)

    tables = (
        jnp.asarray(dft_block(1.0)),
        jnp.asarray(dft_block(length**-1.5)),
        jnp.asarray(twiddles(points)),
    )
    settings = dict(
        compiler_params=pltpu.CompilerParams(vmem_limit_bytes=16 << 20),
        cost_estimate=pl.CostEstimate(
            flops=3 * 2 * 3 * points * SUBLANES * 4 * LANES * LANES,
            bytes_accessed=4 << 20,
            transcendentals=0,
        ),
    )
    scratch = [
        pltpu.VMEM((points, 2, SUBLANES, LANES), f32),
        pltpu.VMEM((2, points * SUBLANES, 2 * LANES), jnp.bfloat16),
        pltpu.VMEM((points * SUBLANES, 2 * LANES), f32),
        pltpu.VMEM((points * SUBLANES, 2 * LANES), f32),
    ]
    result = pl.pallas_call(
        correlate,
        out_shape=jax.ShapeDtypeStruct((count, *block), f32),
        in_specs=[in_vmem] * 4,
        out_specs=in_vmem,
        scratch_shapes=scratch,
        **settings,
    )(got, *tables)
    returned = lax.all_to_all(result, "en", 0, 0, tiled=True)
    mine, give = pl.pallas_call(
        functools.partial(correlate_pieces, 2 * chips),
        out_shape=[jax.ShapeDtypeStruct((chips, *block), f32)] * 2,
        in_specs=[in_vmem] * (2 * chips + 3),
        out_specs=[in_vmem] * 2,
        scratch_shapes=[
            pltpu.VMEM((2 * count, *block), f32),
            pltpu.VMEM((count, *block), f32),
            *scratch,
        ],
        **settings,
    )(*arrived, *tables)
    given = lax.ppermute(give, "en", [(e, e ^ 1) for e in range(count)])
    bundles = pl.pallas_call(
        join_back_kernel,
        out_shape=[bundle] * chips,
        in_specs=[in_vmem] * 2,
        out_specs=[in_vmem] * chips,
        compiler_params=pltpu.CompilerParams(vmem_limit_bytes=4 << 20),
    )(mine, given)
    bundles = list(bundles)
    for z in range(chips - 1, 0, -1):
        bundles[z] = lax.ppermute(bundles[z], "en", [(e, e ^ (2 * z)) for e in range(count)])
    whole = jax.ShapeDtypeStruct(tiled, f32)
    kept = pl.pallas_call(
        keep_first_kernel,
        out_shape=whole,
        in_specs=[in_vmem],
        out_specs=in_hbm,
        scratch_shapes=[pltpu.SemaphoreType.DMA((2,))],
        compiler_params=pltpu.CompilerParams(vmem_limit_bytes=1 << 20),
    )(returned)
    out = pl.pallas_call(
        keep_second_kernel,
        out_shape=whole,
        in_specs=[in_vmem] * chips + [in_hbm],
        out_specs=in_hbm,
        scratch_shapes=[pltpu.SemaphoreType.DMA((chips, 2))],
        input_output_aliases={chips: 0},
        compiler_params=pltpu.CompilerParams(vmem_limit_bytes=1 << 20),
    )(*bundles, kept)
    return out.reshape(2, group_rows, local_len)


def solution(mesh):
    groups = mesh.shape["grp"]
    devices = mesh.devices.reshape(2, groups // 2, mesh.shape["en"])
    finer = Mesh(devices, ("half", "grp", "en"))
    spec = P(None, ("half", "grp"), "en")
    in_specs = (spec, spec, P(("half", "grp")))

    return jax.shard_map(body, mesh=finer, in_specs=in_specs, out_specs=spec, check_vma=False)
```

```python
import functools
import math

import jax
import jax.numpy as jnp
import numpy as np
from jax import lax
from jax.experimental import pallas as pl
from jax.experimental.pallas import tpu as pltpu
from jax.sharding import Mesh
from jax.sharding import PartitionSpec as P

LANES = 128
SUBLANES = 8


def dft_block(scale):
    turn = 2.0 * math.pi / LANES * (np.outer(np.arange(LANES), np.arange(LANES)) % LANES)
    cos, sin = np.cos(turn), np.sin(turn)
    full = (np.block([[cos, -sin], [sin, cos]]) * scale).astype(np.float32)
    high = full.astype(jnp.bfloat16)
    low = (full - high.astype(np.float32)).astype(jnp.bfloat16)
    return np.stack([high, low])


def twiddles(points):
    length = points * LANES
    turn = 2.0 * math.pi / length * (np.outer(np.arange(points), np.arange(LANES)) % length)
    return np.stack([np.cos(turn), -np.sin(turn)]).astype(np.float32)


def times_root(value, numerator, denominator):
    re, im = value
    eighths = 8 * numerator / denominator % 8
    if eighths == 0:
        return re, im
    if eighths == 2:
        return im, -re
    if eighths == 4:
        return -re, -im
    if eighths == 6:
        return -im, re
    half = math.sqrt(0.5)
    if eighths == 1:
        return (re + im) * half, (im - re) * half
    if eighths == 3:
        return (im - re) * half, -(re + im) * half
    turn = 2.0 * math.pi * numerator / denominator
    cos, sin = math.cos(turn), math.sin(turn)
    return re * cos + im * sin, im * cos - re * sin


def add(a, b):
    return a[0] + b[0], a[1] + b[1]


def sub(a, b):
    return a[0] - b[0], a[1] - b[1]


def small_dft(values):
    count = len(values)
    if count == 1:
        return values
    even, odd = small_dft(values[0::2]), small_dft(values[1::2])
    odd = [times_root(v, k, count) for k, v in enumerate(odd)]
    return [add(e, o) for e, o in zip(even, odd)] + [sub(e, o) for e, o in zip(even, odd)]


def long_dft(load, keep, points):
    first = min(8, points)
    second = points // first
    for s in range(second):
        for k, value in enumerate(small_dft([load(e * second + s) for e in range(first)])):
            keep[k * second + s, 0], keep[k * second + s, 1] = times_root(value, s * k, points)
    for k in range(first):
        group = [(keep[k * second + s, 0], keep[k * second + s, 1]) for s in range(second)]
        for j, value in enumerate(small_dft(group)):
            yield k + first * j, value


def split_store(ref, row, rows, re, im):
    for place, part in enumerate((re, im)):
        high = part.astype(jnp.bfloat16)
        low = (part - high.astype(jnp.float32)).astype(jnp.bfloat16)
        ref[0, pl.ds(row, rows), place * LANES : (place + 1) * LANES] = high
        ref[1, pl.ds(row, rows), place * LANES : (place + 1) * LANES] = low


def dot(left, right):
    return jnp.dot(left, right, preferred_element_type=jnp.float32)


def lane_dft(halves, table):
    high, low = halves[0], halves[1]
    return dot(high, table[0]) + dot(low, table[0]) + dot(high, table[1])


def times_twist(twist, k, value):
    re, im = value
    cos, sin = twist[0, pl.ds(k, 1), :], twist[1, pl.ds(k, 1), :]
    return re * cos - im * sin, re * sin + im * cos


def pack_kernel(mirror, lesser, greater, mine, give, second, places, held, first, sems, block_sems):
    _, count, tiles, sub, local_len = lesser.shape
    rows = tiles * sub
    chips = count // 2
    me = lax.axis_index("en")
    loads = [pltpu.make_async_copy(mirror, places, sems.at[0])]
    loads += [pltpu.make_async_copy(greater.at[p], held.at[p], sems.at[1 + p]) for p in range(2)]
    blocks = [
        pltpu.make_async_copy(
            lesser.at[:, me ^ (2 * z + core), 0], target.at[0, z], block_sems.at[core, z]
        )
        for z in range(chips)
        for core, target in enumerate((mine, give))
    ]
    for copy in loads + blocks:
        copy.start()
    loads[0].wait()
    lane = lax.broadcasted_iota(jnp.int32, (rows, count * rows), 1)
    line = lax.broadcasted_iota(jnp.int32, (rows, count * rows), 0)
    goal = jnp.broadcast_to(places[...], (rows, count * rows)) % rows
    source = jnp.where(goal == line, (lane % rows).astype(jnp.float32), 0.0)
    orders = [
        jnp.sum(jnp.where(lane // rows == to, source, 0.0), axis=1, keepdims=True).astype(jnp.int32)
        for to in range(count)
    ]
    for part in range(2):
        loads[1 + part].wait()
        for to in range(count):
            order = jnp.broadcast_to(orders[to], (rows, LANES))
            for start in range(0, local_len, LANES):
                span = slice(start, start + LANES)
                tiles_in = [held[part, to, u, :, span] for u in range(tiles)]
                for t in range(tiles):
                    wanted = order[t * sub : (t + 1) * sub]
                    moved = jnp.zeros((sub, LANES), jnp.float32)
                    for u, tile in enumerate(tiles_in):
                        picked = jnp.take_along_axis(tile, wanted % sub, axis=0)
                        moved = jnp.where(wanted // sub == u, picked, moved)
                    if t == 0:
                        first[to, part, :, span] = moved
                    else:
                        second[to, part, :, span] = moved
    for z in range(chips):
        for core, target in enumerate((mine, give)):
            target[1, z] = first[me ^ (2 * z + core)]
    for copy in blocks:
        copy.wait()


def pack_second_kernel(lesser, second, packed, ready, sems):
    count = second.shape[0]
    own = lax.axis_index("half")
    loads = [
        pltpu.make_async_copy(lesser.at[p, :, 1], ready.at[:, p], sems.at[p]) for p in range(2)
    ]
    stores = [
        pltpu.make_async_copy(second, packed.at[pl.ds((1 - own) * count, count)], sems.at[2]),
        pltpu.make_async_copy(ready, packed.at[pl.ds(own * count, count)], sems.at[3]),
    ]
    for copy in [*loads, stores[0]]:
        copy.start()
    for copy in loads:
        copy.wait()
    stores[1].start()
    for copy in stores:
        copy.wait()


def join_kernel(mine, got, *outs):
    chips = mine.shape[1]
    for t, out in enumerate(outs):
        out[0] = mine[t // chips, t % chips]
        out[1] = got[t // chips, t % chips]


def join_back_kernel(mine, got, *outs):
    for z, out in enumerate(outs):
        out[0] = mine[z]
        out[1] = got[z]


def correlate(got, forward, backward, twist, out, keep, halves, left, right):
    count = got.shape[0] // 2
    rows = got.shape[2]
    steps = got.shape[3] // LANES
    points = count * steps
    own = lax.axis_index("half")

    def read(start, swap):
        def load(t):
            where = slice(t % steps * LANES, (t % steps + 1) * LANES)
            re = got[start + t // steps, 0, :, where]
            im = got[start + t // steps, 1, :, where]
            return (im, re) if swap else (re, im)

        return load

    for which, target in enumerate((left, right)):
        start = jnp.where(own == which, 0, count)
        for k, value in long_dft(read(start, which == 1), keep, points):
            split_store(halves, k * rows, rows, *times_twist(twist, k, value))
        target[...] = lane_dft(halves, forward)

    for k in range(points):
        span = pl.ds(k * rows, rows)
        a_re, a_im = left[span, :LANES], left[span, LANES:]
        b_im, b_re = right[span, :LANES], right[span, LANES:]
        split_store(halves, k * rows, rows, a_re * b_im + a_im * b_re, a_re * b_re - a_im * b_im)
    left[...] = lane_dft(halves, backward)

    def spectrum(k):
        span = pl.ds(k * rows, rows)
        return times_twist(twist, k, (left[span, :LANES], left[span, LANES:]))

    for t, (c_im, c_re) in long_dft(spectrum, keep, points):
        where = slice(t % steps * LANES, (t % steps + 1) * LANES)
        out[t // steps, 0, :, where] = c_im
        out[t // steps, 1, :, where] = -c_re


def send_back(out, mine, give):
    me = lax.axis_index("en")
    for z in range(mine.shape[0]):
        for core, target in enumerate((mine, give)):
            target[z] = out[me ^ (2 * z + core)]


def correlate_whole(got, forward, backward, twist, mine, give, out, *rest):
    correlate(got, forward, backward, twist, out, *rest)
    send_back(out, mine, give)


def correlate_pieces(pieces, *refs):
    blocks, (forward, backward, twist, mine, give) = refs[:pieces], refs[pieces : pieces + 5]
    got, out, *rest = refs[pieces + 5 :]
    chips = pieces // 2
    own = lax.axis_index("half")
    me = lax.axis_index("en")
    for t, block in enumerate(blocks):
        half = own if t < chips else 1 - own
        for core in range(2):
            got[half * (2 * chips) + (me ^ (2 * (t % chips) + core))] = block[core]
    correlate(got, forward, backward, twist, out, *rest)
    send_back(out, mine, give)


def hold_kernel(block, out):
    out[...] = block[...]


def far_first(chips):
    return sorted(range(1, 2 * chips), key=lambda t: (-(t % chips), t < chips))


def keep_kernel(chunk, chips, *refs):
    bundles, out, sems = refs[:chips], refs[-2], refs[-1]
    me = lax.axis_index("en")
    copies = [
        pltpu.make_async_copy(
            bundle.at[core], out.at[:, me ^ (2 * z + core), chunk], sems.at[z, core]
        )
        for z, bundle in enumerate(bundles)
        for core in range(2)
    ]
    for copy in copies:
        copy.start()
    for copy in copies:
        copy.wait()


def body(lesser, greater, mirror):
    _, group_rows, local_len = lesser.shape
    count = lax.axis_size("en")
    rows = group_rows // count
    tiles = rows // SUBLANES
    length = local_len * count
    points = length // LANES
    block = (2, SUBLANES, local_len)
    tiled = (2, count, tiles, SUBLANES, local_len)
    f32 = jnp.float32
    in_vmem = pl.BlockSpec(memory_space=pltpu.VMEM)
    in_smem = pl.BlockSpec(memory_space=pltpu.SMEM)
    in_hbm = pl.BlockSpec(memory_space=pltpu.HBM)

    chips = count // 2
    half_view = (2, chips, *block)
    bundle = jax.ShapeDtypeStruct((2, *block), f32)
    mirror, lesser, greater = (
        pltpu.with_memory_space_constraint(x, pltpu.HBM)
        for x in (mirror[None], lesser.reshape(tiled), greater.reshape(tiled))
    )
    mine, give, second = pl.pallas_call(
        pack_kernel,
        out_shape=[
            jax.ShapeDtypeStruct(half_view, f32),
            jax.ShapeDtypeStruct(half_view, f32),
            jax.ShapeDtypeStruct((count, *block), f32),
        ],
        in_specs=[in_hbm] * 3,
        out_specs=[in_vmem] * 3,
        scratch_shapes=[
            pltpu.VMEM((1, group_rows), jnp.int32),
            pltpu.VMEM(tiled, f32),
            pltpu.VMEM((count, *block), f32),
            pltpu.SemaphoreType.DMA((3,)),
            pltpu.SemaphoreType.DMA((2, chips)),
        ],
        compiler_params=pltpu.CompilerParams(vmem_limit_bytes=8 << 20),
    )(mirror, lesser, greater)
    swap = [(e, e ^ 1) for e in range(count)]

    def join(kernel, mine, given, pieces):
        return list(
            pl.pallas_call(
                kernel,
                out_shape=[bundle] * pieces,
                in_specs=[in_vmem] * 2,
                out_specs=[in_vmem] * pieces,
                compiler_params=pltpu.CompilerParams(vmem_limit_bytes=4 << 20),
            )(mine, given)
        )

    given = lax.ppermute(give, "en", swap)
    packed = pl.pallas_call(
        pack_second_kernel,
        out_shape=jax.ShapeDtypeStruct((2 * count, *block), f32),
        in_specs=[in_hbm, in_vmem],
        out_specs=in_hbm,
        scratch_shapes=[pltpu.VMEM((count, *block), f32), pltpu.SemaphoreType.DMA((4,))],
        compiler_params=pltpu.CompilerParams(vmem_limit_bytes=4 << 20),
    )(lesser, second)
    arrived = join(join_kernel, mine, given, 2 * chips)
    for t in far_first(chips):
        step = t // chips * count + 2 * (t % chips)
        route = [(d, d ^ step) for d in range(2 * count)]
        arrived[t] = lax.ppermute(arrived[t], ("half", "en"), route)
    got = lax.all_to_all(packed, ("half", "en"), 0, 0, tiled=True)

    tables = (
        jnp.asarray(dft_block(1.0)),
        jnp.asarray(dft_block(length**-1.5)),
        jnp.asarray(twiddles(points)),
    )
    settings = dict(
        compiler_params=pltpu.CompilerParams(vmem_limit_bytes=16 << 20),
        cost_estimate=pl.CostEstimate(
            flops=3 * 2 * 3 * points * SUBLANES * 4 * LANES * LANES,
            bytes_accessed=4 << 20,
            transcendentals=0,
        ),
    )
    scratch = [
        pltpu.VMEM((points, 2, SUBLANES, LANES), f32),
        pltpu.VMEM((2, points * SUBLANES, 2 * LANES), jnp.bfloat16),
        pltpu.VMEM((points * SUBLANES, 2 * LANES), f32),
        pltpu.VMEM((points * SUBLANES, 2 * LANES), f32),
    ]
    piece = jax.ShapeDtypeStruct((chips, *block), f32)
    first = pl.pallas_call(
        functools.partial(correlate_pieces, 2 * chips),
        out_shape=[piece] * 2,
        in_specs=[in_vmem] * (2 * chips + 3),
        out_specs=[in_vmem] * 2,
        scratch_shapes=[
            pltpu.VMEM((2 * count, *block), f32),
            pltpu.VMEM((count, *block), f32),
            *scratch,
        ],
        **settings,
    )(*arrived, *tables)
    second = pl.pallas_call(
        correlate_whole,
        out_shape=[piece] * 2,
        in_specs=[in_vmem] * 4,
        out_specs=[in_vmem] * 2,
        scratch_shapes=[pltpu.VMEM((count, *block), f32), *scratch],
        **settings,
    )(got, *tables)
    out = []
    for chunk, (name, (mine, give)) in enumerate({"a": first, "b": second}.items()):
        given = lax.ppermute(give, "en", swap)
        bundles = join(join_back_kernel, mine, given, chips)
        for z in range(chips - 1, 0, -1):
            route = [(e, e ^ (2 * z)) for e in range(count)]
            bundles[z] = lax.ppermute(bundles[z], "en", route)
        if name == "a":
            bundles[0] = pl.pallas_call(
                hold_kernel,
                out_shape=bundle,
                in_specs=[in_vmem],
                out_specs=in_vmem,
                compiler_params=pltpu.CompilerParams(vmem_limit_bytes=1 << 20),
            )(bundles[0])
        out = [
            pl.pallas_call(
                functools.partial(keep_kernel, chunk, chips),
                out_shape=jax.ShapeDtypeStruct(tiled, f32),
                in_specs=[in_vmem] * chips + [in_hbm] * len(out),
                out_specs=in_hbm,
                scratch_shapes=[pltpu.SemaphoreType.DMA((chips, 2))],
                input_output_aliases={chips: 0} if out else {},
                compiler_params=pltpu.CompilerParams(vmem_limit_bytes=1 << 20),
            )(*bundles, *out)
        ]
    return out[0].reshape(2, group_rows, local_len)


def solution(mesh):
    groups = mesh.shape["grp"]
    devices = mesh.devices.reshape(2, groups // 2, mesh.shape["en"])
    finer = Mesh(devices, ("half", "grp", "en"))
    spec = P(None, ("half", "grp"), "en")
    in_specs = (spec, spec, P(("half", "grp")))

    return jax.shard_map(body, mesh=finer, in_specs=in_specs, out_specs=spec, check_vma=False)
```

```python
import functools
import math

import jax
import jax.numpy as jnp
import numpy as np
from jax import lax
from jax.experimental import pallas as pl
from jax.experimental.pallas import tpu as pltpu
from jax.sharding import Mesh
from jax.sharding import PartitionSpec as P

LANES = 128
SUBLANES = 8


def dft_block(scale):
    turn = 2.0 * math.pi / LANES * (np.outer(np.arange(LANES), np.arange(LANES)) % LANES)
    cos, sin = np.cos(turn), np.sin(turn)
    full = (np.block([[cos, -sin], [sin, cos]]) * scale).astype(np.float32)
    high = full.astype(jnp.bfloat16)
    low = (full - high.astype(np.float32)).astype(jnp.bfloat16)
    return np.stack([high, low])


def twiddles(points):
    length = points * LANES
    turn = 2.0 * math.pi / length * (np.outer(np.arange(points), np.arange(LANES)) % length)
    return np.stack([np.cos(turn), -np.sin(turn)]).astype(np.float32)


def times_root(value, numerator, denominator):
    re, im = value
    eighths = 8 * numerator / denominator % 8
    if eighths == 0:
        return re, im
    if eighths == 2:
        return im, -re
    if eighths == 4:
        return -re, -im
    if eighths == 6:
        return -im, re
    half = math.sqrt(0.5)
    if eighths == 1:
        return (re + im) * half, (im - re) * half
    if eighths == 3:
        return (im - re) * half, -(re + im) * half
    turn = 2.0 * math.pi * numerator / denominator
    cos, sin = math.cos(turn), math.sin(turn)
    return re * cos + im * sin, im * cos - re * sin


def add(a, b):
    return a[0] + b[0], a[1] + b[1]


def sub(a, b):
    return a[0] - b[0], a[1] - b[1]


def small_dft(values):
    count = len(values)
    if count == 1:
        return values
    even, odd = small_dft(values[0::2]), small_dft(values[1::2])
    odd = [times_root(v, k, count) for k, v in enumerate(odd)]
    return [add(e, o) for e, o in zip(even, odd)] + [sub(e, o) for e, o in zip(even, odd)]


def long_dft(load, keep, points):
    first = min(8, points)
    second = points // first
    for s in range(second):
        for k, value in enumerate(small_dft([load(e * second + s) for e in range(first)])):
            keep[k * second + s, 0], keep[k * second + s, 1] = times_root(value, s * k, points)
    for k in range(first):
        group = [(keep[k * second + s, 0], keep[k * second + s, 1]) for s in range(second)]
        for j, value in enumerate(small_dft(group)):
            yield k + first * j, value


def split_store(ref, row, rows, re, im):
    for place, part in enumerate((re, im)):
        high = part.astype(jnp.bfloat16)
        low = (part - high.astype(jnp.float32)).astype(jnp.bfloat16)
        ref[0, pl.ds(row, rows), place * LANES : (place + 1) * LANES] = high
        ref[1, pl.ds(row, rows), place * LANES : (place + 1) * LANES] = low


def dot(left, right):
    return jnp.dot(left, right, preferred_element_type=jnp.float32)


def lane_dft(halves, table):
    high, low = halves[0], halves[1]
    return dot(high, table[0]) + dot(low, table[0]) + dot(high, table[1])


def times_twist(twist, k, value):
    re, im = value
    cos, sin = twist[0, pl.ds(k, 1), :], twist[1, pl.ds(k, 1), :]
    return re * cos - im * sin, re * sin + im * cos


def pack_kernel(units, alone, mirror, lesser, greater, mine, give, *refs):
    *single, places, held, moved_rows, sems, block_sems = refs
    _, count, tiles, sub, local_len = lesser.shape
    rows = tiles * sub
    me = lax.axis_index("en")
    loads = [pltpu.make_async_copy(mirror, places, sems.at[0])]
    loads += [pltpu.make_async_copy(greater.at[p], held.at[p], sems.at[1 + p]) for p in range(2)]
    offers = [(mine.at[i], *unit, 0) for i, unit in enumerate(units)]
    offers += [(give.at[i], *unit, 1) for i, unit in enumerate(units)]
    offers += [(ref, *one) for ref, one in zip(single, alone)]
    blocks = [
        pltpu.make_async_copy(lesser.at[:, me ^ (2 * chip + core), chunk], ref, block_sems.at[i])
        for i, (ref, chunk, (half, chip), core) in enumerate(offers)
        if not half
    ]
    for copy in loads + blocks:
        copy.start()
    loads[0].wait()
    lane = lax.broadcasted_iota(jnp.int32, (rows, count * rows), 1)
    line = lax.broadcasted_iota(jnp.int32, (rows, count * rows), 0)
    goal = jnp.broadcast_to(places[...], (rows, count * rows)) % rows
    source = jnp.where(goal == line, (lane % rows).astype(jnp.float32), 0.0)
    orders = [
        jnp.sum(jnp.where(lane // rows == to, source, 0.0), axis=1, keepdims=True).astype(jnp.int32)
        for to in range(count)
    ]
    for part in range(2):
        loads[1 + part].wait()
        for to in range(count):
            order = jnp.broadcast_to(orders[to], (rows, LANES))
            for start in range(0, local_len, LANES):
                span = slice(start, start + LANES)
                tiles_in = [held[part, to, u, :, span] for u in range(tiles)]
                for t in range(tiles):
                    wanted = order[t * sub : (t + 1) * sub]
                    moved = jnp.zeros((sub, LANES), jnp.float32)
                    for u, tile in enumerate(tiles_in):
                        picked = jnp.take_along_axis(tile, wanted % sub, axis=0)
                        moved = jnp.where(wanted // sub == u, picked, moved)
                    moved_rows[t, to, part, :, span] = moved
    for ref, chunk, (half, chip), core in offers:
        if half:
            ref[...] = moved_rows[chunk, me ^ (2 * chip + core)]
    for copy in blocks:
        copy.wait()


def join_kernel(groups, *refs):
    outs = refs[-len(groups) :]
    for group, out in zip(groups, outs):
        for i, (which, index) in enumerate(group):
            out[2 * i] = refs[2 * which][index]
            out[2 * i + 1] = refs[2 * which + 1][index]


def correlate(got, forward, backward, twist, out, keep, halves, left, right):
    count = got.shape[0] // 2
    rows = got.shape[2]
    steps = got.shape[3] // LANES
    points = count * steps
    own = lax.axis_index("half")

    def read(start, swap):
        def load(t):
            where = slice(t % steps * LANES, (t % steps + 1) * LANES)
            re = got[start + t // steps, 0, :, where]
            im = got[start + t // steps, 1, :, where]
            return (im, re) if swap else (re, im)

        return load

    for which, target in enumerate((left, right)):
        start = jnp.where(own == which, 0, count)
        for k, value in long_dft(read(start, which == 1), keep, points):
            split_store(halves, k * rows, rows, *times_twist(twist, k, value))
        target[...] = lane_dft(halves, forward)

    for k in range(points):
        span = pl.ds(k * rows, rows)
        a_re, a_im = left[span, :LANES], left[span, LANES:]
        b_im, b_re = right[span, :LANES], right[span, LANES:]
        split_store(halves, k * rows, rows, a_re * b_im + a_im * b_re, a_re * b_re - a_im * b_im)
    left[...] = lane_dft(halves, backward)

    def spectrum(k):
        span = pl.ds(k * rows, rows)
        return times_twist(twist, k, (left[span, :LANES], left[span, LANES:]))

    for t, (c_im, c_re) in long_dft(spectrum, keep, points):
        where = slice(t % steps * LANES, (t % steps + 1) * LANES)
        out[t // steps, 0, :, where] = c_im
        out[t // steps, 1, :, where] = -c_re


def pieces_of(refs, held):
    for ref, blocks in zip(refs, held):
        for i, block in enumerate(blocks):
            yield (ref.at[i] if len(blocks) > 1 else ref), *block


def correlate_kernel(chunk, held, bundled, direct, *refs):
    count = len(held)
    pieces, (forward, backward, twist) = refs[:count], refs[count : count + 3]
    mine, give, *rest = refs[count + 3 :]
    far, (got, out, *scratch) = rest[: 2 * len(direct)], rest[2 * len(direct) :]
    own = lax.axis_index("half")
    me = lax.axis_index("en")
    for ref, of, (half, chip), core in pieces_of(pieces, held):
        if of == chunk:
            side = 1 - own if half else own
            got[side * out.shape[0] + (me ^ (2 * chip + core))] = ref[...]
    correlate(got, forward, backward, twist, out, *scratch)
    for i, chip in enumerate(bundled):
        mine[i] = out[me ^ (2 * chip)]
        give[i] = out[me ^ (2 * chip + 1)]
    for i, ref in enumerate(far):
        ref[...] = out[me ^ (2 * direct[i // 2] + i % 2)]


def keep_kernel(held, *refs):
    out, sems = refs[-2:]
    me = lax.axis_index("en")
    copies = [
        pltpu.make_async_copy(ref, out.at[:, me ^ (2 * chip + core), chunk], sems.at[i])
        for i, (ref, chunk, chip, core) in enumerate(pieces_of(refs, held))
    ]
    for copy in copies:
        copy.start()
    for copy in copies:
        copy.wait()


def call(kernel, out_shape, in_specs, out_specs, scratch=(), mib=4, **settings):
    return pl.pallas_call(
        kernel,
        out_shape=out_shape,
        in_specs=in_specs,
        out_specs=out_specs,
        scratch_shapes=scratch,
        compiler_params=pltpu.CompilerParams(vmem_limit_bytes=mib << 20),
        **settings,
    )


def plan(chips):
    arrive = [(half, chip) for chip in range(chips - 1, -1, -1) for half in (1, 0)]
    back = list(range(chips - 1, -1, -1))
    cut = chips // 2
    return arrive[: 2 * cut], arrive[2 * cut :], back[:cut], back[cut:]


def body(lesser, greater, mirror):
    _, group_rows, local_len = lesser.shape
    count = lax.axis_size("en")
    chips = count // 2
    rows = group_rows // count
    tiles = rows // SUBLANES
    length = local_len * count
    points = length // LANES
    f32 = jnp.float32
    block = jax.ShapeDtypeStruct((2, SUBLANES, local_len), f32)
    tiled = jax.ShapeDtypeStruct((2, count, tiles, SUBLANES, local_len), f32)
    in_vmem = pl.BlockSpec(memory_space=pltpu.VMEM)
    in_hbm = pl.BlockSpec(memory_space=pltpu.HBM)
    dma = pltpu.SemaphoreType.DMA
    far, near, far_back, near_back = plan(chips)

    def stack(pieces):
        return jax.ShapeDtypeStruct((pieces, *block.shape), f32)

    def vmem(shape):
        return pltpu.VMEM(shape.shape, shape.dtype)

    def swap(give):
        return lax.ppermute(give, "en", [(e, e ^ 1) for e in range(count)])

    def join(pairs, groups):
        shapes = [stack(2 * len(group)) for group in groups]
        return call(
            functools.partial(join_kernel, groups),
            shapes,
            [in_vmem] * 2 * len(pairs),
            [in_vmem] * len(groups),
        )(*sum(pairs, ()))

    def send(value, half, chip, core=0):
        distance = half * count + 2 * chip + core
        route = [(d, d ^ distance) for d in range(2 * count)]
        return lax.ppermute(value, ("half", "en"), route) if distance else value

    mirror, lesser, greater = (
        pltpu.with_memory_space_constraint(x, pltpu.HBM)
        for x in (mirror[None], lesser.reshape(tiled.shape), greater.reshape(tiled.shape))
    )
    tables = (
        jnp.asarray(dft_block(1.0)),
        jnp.asarray(dft_block(length**-1.5)),
        jnp.asarray(twiddles(points)),
    )

    last = tiles - 1
    chunks = range(tiles)
    alone = [(0, t, core) for t in far[:1] for core in range(2)]
    groups = [[(0, t)] for t in far[1:]]
    groups += [[(chunk, t) for chunk in chunks] for t in near]
    groups += [[(chunk, t)] for chunk in chunks[1:] for t in far]
    units = sum(groups, [])
    mine, give, *single = call(
        functools.partial(pack_kernel, units, alone),
        [stack(len(units))] * 2 + [block] * len(alone),
        [in_hbm] * 3,
        [in_vmem] * (2 + len(alone)),
        [
            pltpu.VMEM((1, group_rows), jnp.int32),
            vmem(tiled),
            pltpu.VMEM((tiles, count, *block.shape), f32),
            dma((3,)),
            dma((2 * len(units) + len(alone),)),
        ],
        mib=8,
    )(mirror, lesser, greater)
    given = swap(give)
    arrived = [send(value, *t, core) for value, (_, t, core) in zip(single, alone)]
    held = [(one,) for one in alone]
    places = iter(range(len(units)))
    joined = join([(mine, given)], [[(0, next(places)) for _ in group] for group in groups])
    for value, group in zip(joined, groups):
        chunk, t = group[0]
        arrived.append(send(value, *t))
        held.append(tuple((*unit, core) for unit in group for core in range(2)))

    kept, pairs, out = [], [], []
    for chunk in chunks:
        direct = far_back[:1] if chunk == last else []
        bundled = far_back[len(direct) :] + near_back
        used = [i for i, blocks in enumerate(held) if any(b[0] == chunk for b in blocks)]
        mine, give, *single = call(
            functools.partial(
                correlate_kernel, chunk, tuple(held[i] for i in used), bundled, direct
            ),
            [stack(len(bundled))] * 2 + [block] * 2 * len(direct),
            [in_vmem] * (len(used) + 3),
            [in_vmem] * (2 + 2 * len(direct)),
            [
                vmem(stack(2 * count)),
                vmem(stack(count)),
                pltpu.VMEM((points, 2, SUBLANES, LANES), f32),
                pltpu.VMEM((2, points * SUBLANES, 2 * LANES), jnp.bfloat16),
                pltpu.VMEM((points * SUBLANES, 2 * LANES), f32),
                pltpu.VMEM((points * SUBLANES, 2 * LANES), f32),
            ],
            mib=16,
            cost_estimate=pl.CostEstimate(
                flops=3 * 2 * 3 * points * SUBLANES * 4 * LANES * LANES,
                bytes_accessed=4 << 20,
                transcendentals=0,
            ),
        )(*(arrived[i] for i in used), *tables)
        returned = [
            (
                send(value, 0, direct[i // 2], i % 2),
                ((chunk, direct[i // 2], i % 2),),
            )
            for i, value in enumerate(single)
        ]
        pairs.append((mine, swap(give)))
        kept.append(bundled)
        groups = [[(chunk, z)] for z in far_back[len(direct) :]]
        if chunk == last:
            groups += [[(c, z) for c in chunks] for z in near_back]
        joined = join(
            pairs if chunk == last else pairs[-1:],
            [[(c if chunk == last else 0, kept[c].index(z)) for c, z in group] for group in groups],
        )
        for value, group in zip(joined, groups):
            z = group[0][1]
            blocks = tuple((*unit, core) for unit in group for core in range(2))
            returned.append((send(value, 0, z), blocks))
        values, blocks = zip(*returned)
        out = [
            call(
                functools.partial(keep_kernel, blocks),
                tiled,
                [in_vmem] * len(values) + [in_hbm] * len(out),
                in_hbm,
                [dma((sum(map(len, blocks)),))],
                mib=1,
                input_output_aliases={len(values): 0} if out else {},
            )(*values, *out)
        ]
    return out[0].reshape(2, group_rows, local_len)


def solution(mesh):
    groups = mesh.shape["grp"]
    devices = mesh.devices.reshape(2, groups // 2, mesh.shape["en"])
    finer = Mesh(devices, ("half", "grp", "en"))
    spec = P(None, ("half", "grp"), "en")
    in_specs = (spec, spec, P(("half", "grp")))

    return jax.shard_map(body, mesh=finer, in_specs=in_specs, out_specs=spec, check_vma=False)
```

```python
import functools
import math

import jax
import jax.numpy as jnp
import numpy as np
from jax import lax
from jax.experimental import pallas as pl
from jax.experimental.pallas import tpu as pltpu
from jax.sharding import Mesh
from jax.sharding import PartitionSpec as P

LANES = 128
SUBLANES = 8


def dft_block(scale):
    turn = 2.0 * math.pi / LANES * (np.outer(np.arange(LANES), np.arange(LANES)) % LANES)
    cos, sin = np.cos(turn), np.sin(turn)
    full = (np.block([[cos, -sin], [sin, cos]]) * scale).astype(np.float32)
    high = full.astype(jnp.bfloat16)
    low = (full - high.astype(np.float32)).astype(jnp.bfloat16)
    return np.stack([high, low])


def twiddles(points):
    length = points * LANES
    turn = 2.0 * math.pi / length * (np.outer(np.arange(points), np.arange(LANES)) % length)
    return np.stack([np.cos(turn), -np.sin(turn)]).astype(np.float32)


def times_root(value, numerator, denominator):
    re, im = value
    eighths = 8 * numerator / denominator % 8
    if eighths == 0:
        return re, im
    if eighths == 2:
        return im, -re
    if eighths == 4:
        return -re, -im
    if eighths == 6:
        return -im, re
    half = math.sqrt(0.5)
    if eighths == 1:
        return (re + im) * half, (im - re) * half
    if eighths == 3:
        return (im - re) * half, -(re + im) * half
    turn = 2.0 * math.pi * numerator / denominator
    cos, sin = math.cos(turn), math.sin(turn)
    return re * cos + im * sin, im * cos - re * sin


def add(a, b):
    return a[0] + b[0], a[1] + b[1]


def sub(a, b):
    return a[0] - b[0], a[1] - b[1]


def small_dft(values):
    count = len(values)
    if count == 1:
        return values
    even, odd = small_dft(values[0::2]), small_dft(values[1::2])
    odd = [times_root(v, k, count) for k, v in enumerate(odd)]
    return [add(e, o) for e, o in zip(even, odd)] + [sub(e, o) for e, o in zip(even, odd)]


def long_dft(load, keep, points):
    first = min(8, points)
    second = points // first
    for s in range(second):
        for k, value in enumerate(small_dft([load(e * second + s) for e in range(first)])):
            keep[k * second + s, 0], keep[k * second + s, 1] = times_root(value, s * k, points)
    for k in range(first):
        group = [(keep[k * second + s, 0], keep[k * second + s, 1]) for s in range(second)]
        for j, value in enumerate(small_dft(group)):
            yield k + first * j, value


def split_store(ref, row, rows, re, im):
    for place, part in enumerate((re, im)):
        high = part.astype(jnp.bfloat16)
        low = (part - high.astype(jnp.float32)).astype(jnp.bfloat16)
        ref[0, pl.ds(row, rows), place * LANES : (place + 1) * LANES] = high
        ref[1, pl.ds(row, rows), place * LANES : (place + 1) * LANES] = low


def dot(left, right):
    return jnp.dot(left, right, preferred_element_type=jnp.float32)


def lane_dft(halves, table):
    high, low = halves[0], halves[1]
    return dot(high, table[0]) + dot(low, table[0]) + dot(high, table[1])


def times_twist(twist, k, value):
    re, im = value
    cos, sin = twist[0, pl.ds(k, 1), :], twist[1, pl.ds(k, 1), :]
    return re * cos - im * sin, re * sin + im * cos


def device(me, count, turn, core):
    chips = count // 2
    return 2 * lax.rem(lax.div(me, 2) + turn % chips, chips) + (lax.rem(me, 2) ^ core)


def pack_kernel(units, alone, mirror, lesser, greater, mine, give, *refs):
    *single, places, held, moved_rows, sems, block_sems = refs
    _, count, tiles, sub, local_len = lesser.shape
    rows = tiles * sub
    me = lax.axis_index("en")
    loads = [pltpu.make_async_copy(mirror, places, sems.at[0])]
    loads += [pltpu.make_async_copy(greater.at[p], held.at[p], sems.at[1 + p]) for p in range(2)]
    offers = [(mine.at[i], *unit, 0) for i, unit in enumerate(units)]
    offers += [(give.at[i], *unit, 1) for i, unit in enumerate(units)]
    offers += [(ref, *one) for ref, one in zip(single, alone)]
    blocks = [
        pltpu.make_async_copy(
            lesser.at[:, device(me, count, turn, core), chunk], ref, block_sems.at[i]
        )
        for i, (ref, chunk, (half, turn), core) in enumerate(offers)
        if not half
    ]
    for copy in loads + blocks:
        copy.start()
    loads[0].wait()
    lane = lax.broadcasted_iota(jnp.int32, (rows, count * rows), 1)
    line = lax.broadcasted_iota(jnp.int32, (rows, count * rows), 0)
    goal = jnp.broadcast_to(places[...], (rows, count * rows)) % rows
    source = jnp.where(goal == line, (lane % rows).astype(jnp.float32), 0.0)
    orders = [
        jnp.sum(jnp.where(lane // rows == to, source, 0.0), axis=1, keepdims=True).astype(jnp.int32)
        for to in range(count)
    ]
    for part in range(2):
        loads[1 + part].wait()
        for to in range(count):
            order = jnp.broadcast_to(orders[to], (rows, LANES))
            for start in range(0, local_len, LANES):
                span = slice(start, start + LANES)
                tiles_in = [held[part, to, u, :, span] for u in range(tiles)]
                for t in range(tiles):
                    wanted = order[t * sub : (t + 1) * sub]
                    moved = jnp.zeros((sub, LANES), jnp.float32)
                    for u, tile in enumerate(tiles_in):
                        picked = jnp.take_along_axis(tile, wanted % sub, axis=0)
                        moved = jnp.where(wanted // sub == u, picked, moved)
                    moved_rows[t, to, part, :, span] = moved
    for ref, chunk, (half, turn), core in offers:
        if half:
            ref[...] = moved_rows[chunk, device(me, count, turn, core)]
    for copy in blocks:
        copy.wait()


def join_kernel(groups, *refs):
    outs = refs[-len(groups) :]
    for group, out in zip(groups, outs):
        for i, (which, index) in enumerate(group):
            out[2 * i] = refs[2 * which][index]
            out[2 * i + 1] = refs[2 * which + 1][index]


def correlate(got, forward, backward, twist, out, keep, halves, left, right):
    count = got.shape[0] // 2
    rows = got.shape[2]
    steps = got.shape[3] // LANES
    points = count * steps
    own = lax.axis_index("half")

    def read(start, swap):
        def load(t):
            where = slice(t % steps * LANES, (t % steps + 1) * LANES)
            re = got[start + t // steps, 0, :, where]
            im = got[start + t // steps, 1, :, where]
            return (im, re) if swap else (re, im)

        return load

    for which, target in enumerate((left, right)):
        start = jnp.where(own == which, 0, count)
        for k, value in long_dft(read(start, which == 1), keep, points):
            split_store(halves, k * rows, rows, *times_twist(twist, k, value))
        target[...] = lane_dft(halves, forward)

    for k in range(points):
        span = pl.ds(k * rows, rows)
        a_re, a_im = left[span, :LANES], left[span, LANES:]
        b_im, b_re = right[span, :LANES], right[span, LANES:]
        split_store(halves, k * rows, rows, a_re * b_im + a_im * b_re, a_re * b_re - a_im * b_im)
    left[...] = lane_dft(halves, backward)

    def spectrum(k):
        span = pl.ds(k * rows, rows)
        return times_twist(twist, k, (left[span, :LANES], left[span, LANES:]))

    for t, (c_im, c_re) in long_dft(spectrum, keep, points):
        where = slice(t % steps * LANES, (t % steps + 1) * LANES)
        out[t // steps, 0, :, where] = c_im
        out[t // steps, 1, :, where] = -c_re


def pieces_of(refs, held):
    for ref, blocks in zip(refs, held):
        for i, block in enumerate(blocks):
            yield (ref.at[i] if len(blocks) > 1 else ref), *block


def correlate_kernel(chunk, held, bundled, direct, *refs):
    pieces, (forward, backward, twist) = refs[: len(held)], refs[len(held) : len(held) + 3]
    mine, give, *rest = refs[len(held) + 3 :]
    far, (got, out, *scratch) = rest[: 2 * len(direct)], rest[2 * len(direct) :]
    count = out.shape[0]
    own = lax.axis_index("half")
    me = lax.axis_index("en")
    for ref, of, (half, turn), core in pieces_of(pieces, held):
        if of == chunk:
            side = 1 - own if half else own
            got[side * count + device(me, count, -turn, core)] = ref[...]
    correlate(got, forward, backward, twist, out, *scratch)
    for i, turn in enumerate(bundled):
        mine[i] = out[device(me, count, turn, 0)]
        give[i] = out[device(me, count, turn, 1)]
    for i, ref in enumerate(far):
        ref[...] = out[device(me, count, direct[i // 2], i % 2)]


def keep_kernel(held, *refs):
    out, sems = refs[-2:]
    count = out.shape[1]
    me = lax.axis_index("en")
    copies = [
        pltpu.make_async_copy(ref, out.at[:, device(me, count, -turn, core), chunk], sems.at[i])
        for i, (ref, chunk, turn, core) in enumerate(pieces_of(refs, held))
    ]
    for copy in copies:
        copy.start()
    for copy in copies:
        copy.wait()


def call(kernel, out_shape, in_specs, out_specs, scratch=(), mib=4, **settings):
    return pl.pallas_call(
        kernel,
        out_shape=out_shape,
        in_specs=in_specs,
        out_specs=out_specs,
        scratch_shapes=scratch,
        compiler_params=pltpu.CompilerParams(vmem_limit_bytes=mib << 20),
        **settings,
    )


def plan(chips):
    turns = sorted(range(1, chips), key=lambda turn: (-min(turn, chips - turn), turn))
    arrive = [(half, turn) for turn in turns for half in (1, 0)]
    return arrive, [(1, 0), (0, 0)], list(range(1, chips)), [0]


def body(lesser, greater, mirror):
    _, group_rows, local_len = lesser.shape
    count = lax.axis_size("en")
    chips = count // 2
    rows = group_rows // count
    tiles = rows // SUBLANES
    length = local_len * count
    points = length // LANES
    f32 = jnp.float32
    block = jax.ShapeDtypeStruct((2, SUBLANES, local_len), f32)
    tiled = jax.ShapeDtypeStruct((2, count, tiles, SUBLANES, local_len), f32)
    in_vmem = pl.BlockSpec(memory_space=pltpu.VMEM)
    in_hbm = pl.BlockSpec(memory_space=pltpu.HBM)
    dma = pltpu.SemaphoreType.DMA
    far, near, far_back, near_back = plan(chips)

    def stack(pieces):
        return jax.ShapeDtypeStruct((pieces, *block.shape), f32)

    def vmem(shape):
        return pltpu.VMEM(shape.shape, shape.dtype)

    def swap(give):
        return lax.ppermute(give, "en", [(e, e ^ 1) for e in range(count)])

    def join(pairs, groups):
        shapes = [stack(2 * len(group)) for group in groups]
        return call(
            functools.partial(join_kernel, groups),
            shapes,
            [in_vmem] * 2 * len(pairs),
            [in_vmem] * len(groups),
        )(*sum(pairs, ()))

    def send(value, half, turn, core=0):
        if not half + turn + core:
            return value
        pairs = [(h, z, c) for h in range(2) for z in range(chips) for c in range(2)]
        route = [
            (h * count + 2 * z + c, (h ^ half) * count + 2 * ((z + turn) % chips) + (c ^ core))
            for h, z, c in pairs
        ]
        return lax.ppermute(value, ("half", "en"), route)

    mirror, lesser, greater = (
        pltpu.with_memory_space_constraint(x, pltpu.HBM)
        for x in (mirror[None], lesser.reshape(tiled.shape), greater.reshape(tiled.shape))
    )
    tables = (
        jnp.asarray(dft_block(1.0)),
        jnp.asarray(dft_block(length**-1.5)),
        jnp.asarray(twiddles(points)),
    )

    last = tiles - 1
    chunks = range(tiles)
    alone = [(0, t, core) for t in far[:1] for core in range(2)]
    groups = [[(0, t)] for t in far[1:]]
    groups += [[(chunk, t) for chunk in chunks] for t in near]
    groups += [[(chunk, t)] for chunk in chunks[1:] for t in far]
    units = sum(groups, [])
    mine, give, *single = call(
        functools.partial(pack_kernel, units, alone),
        [stack(len(units))] * 2 + [block] * len(alone),
        [in_hbm] * 3,
        [in_vmem] * (2 + len(alone)),
        [
            pltpu.VMEM((1, group_rows), jnp.int32),
            vmem(tiled),
            pltpu.VMEM((tiles, count, *block.shape), f32),
            dma((3,)),
            dma((2 * len(units) + len(alone),)),
        ],
        mib=8,
    )(mirror, lesser, greater)
    given = swap(give)
    arrived = [send(value, *t, core) for value, (_, t, core) in zip(single, alone)]
    held = [(one,) for one in alone]
    places = iter(range(len(units)))
    joined = join([(mine, given)], [[(0, next(places)) for _ in group] for group in groups])
    for value, group in zip(joined, groups):
        chunk, t = group[0]
        arrived.append(send(value, *t))
        held.append(tuple((*unit, core) for unit in group for core in range(2)))

    kept, pairs, out = [], [], []
    for chunk in chunks:
        direct = far_back[:1] if chunk == last else []
        bundled = far_back[len(direct) :] + near_back
        used = [i for i, blocks in enumerate(held) if any(b[0] == chunk for b in blocks)]
        mine, give, *single = call(
            functools.partial(
                correlate_kernel, chunk, tuple(held[i] for i in used), bundled, direct
            ),
            [stack(len(bundled))] * 2 + [block] * 2 * len(direct),
            [in_vmem] * (len(used) + 3),
            [in_vmem] * (2 + 2 * len(direct)),
            [
                vmem(stack(2 * count)),
                vmem(stack(count)),
                pltpu.VMEM((points, 2, SUBLANES, LANES), f32),
                pltpu.VMEM((2, points * SUBLANES, 2 * LANES), jnp.bfloat16),
                pltpu.VMEM((points * SUBLANES, 2 * LANES), f32),
                pltpu.VMEM((points * SUBLANES, 2 * LANES), f32),
            ],
            mib=16,
            cost_estimate=pl.CostEstimate(
                flops=3 * 2 * 3 * points * SUBLANES * 4 * LANES * LANES,
                bytes_accessed=4 << 20,
                transcendentals=0,
            ),
        )(*(arrived[i] for i in used), *tables)
        returned = [
            (
                send(value, 0, direct[i // 2], i % 2),
                ((chunk, direct[i // 2], i % 2),),
            )
            for i, value in enumerate(single)
        ]
        pairs.append((mine, swap(give)))
        kept.append(bundled)
        groups = [[(chunk, z)] for z in far_back[len(direct) :]]
        if chunk == last:
            groups += [[(c, z) for c in chunks] for z in near_back]
        joined = join(
            pairs if chunk == last else pairs[-1:],
            [[(c if chunk == last else 0, kept[c].index(z)) for c, z in group] for group in groups],
        )
        for value, group in zip(joined, groups):
            z = group[0][1]
            blocks = tuple((*unit, core) for unit in group for core in range(2))
            returned.append((send(value, 0, z), blocks))
        values, blocks = zip(*returned)
        out = [
            call(
                functools.partial(keep_kernel, blocks),
                tiled,
                [in_vmem] * len(values) + [in_hbm] * len(out),
                in_hbm,
                [dma((sum(map(len, blocks)),))],
                mib=1,
                input_output_aliases={len(values): 0} if out else {},
            )(*values, *out)
        ]
    return out[0].reshape(2, group_rows, local_len)


def solution(mesh):
    groups = mesh.shape["grp"]
    devices = mesh.devices.reshape(2, groups // 2, mesh.shape["en"])
    finer = Mesh(devices, ("half", "grp", "en"))
    spec = P(None, ("half", "grp"), "en")
    in_specs = (spec, spec, P(("half", "grp")))

    return jax.shard_map(body, mesh=finer, in_specs=in_specs, out_specs=spec, check_vma=False)
```

```python
import functools
import math

import jax
import jax.numpy as jnp
import numpy as np
from jax import lax
from jax.experimental import pallas as pl
from jax.experimental.pallas import tpu as pltpu
from jax.sharding import Mesh
from jax.sharding import PartitionSpec as P

LANES = 128
SUBLANES = 8


def dft_block(scale):
    turn = 2.0 * math.pi / LANES * (np.outer(np.arange(LANES), np.arange(LANES)) % LANES)
    cos, sin = np.cos(turn), np.sin(turn)
    full = (np.block([[cos, -sin], [sin, cos]]) * scale).astype(np.float32)
    high = full.astype(jnp.bfloat16)
    low = (full - high.astype(np.float32)).astype(jnp.bfloat16)
    return np.stack([high, low])


def twiddles(points):
    length = points * LANES
    turn = 2.0 * math.pi / length * (np.outer(np.arange(points), np.arange(LANES)) % length)
    return np.stack([np.cos(turn), -np.sin(turn)]).astype(np.float32)


def times_root(value, numerator, denominator):
    re, im = value
    eighths = 8 * numerator / denominator % 8
    if eighths == 0:
        return re, im
    if eighths == 2:
        return im, -re
    if eighths == 4:
        return -re, -im
    if eighths == 6:
        return -im, re
    half = math.sqrt(0.5)
    if eighths == 1:
        return (re + im) * half, (im - re) * half
    if eighths == 3:
        return (im - re) * half, -(re + im) * half
    turn = 2.0 * math.pi * numerator / denominator
    cos, sin = math.cos(turn), math.sin(turn)
    return re * cos + im * sin, im * cos - re * sin


def add(a, b):
    return a[0] + b[0], a[1] + b[1]


def sub(a, b):
    return a[0] - b[0], a[1] - b[1]


def small_dft(values):
    count = len(values)
    if count == 1:
        return values
    even, odd = small_dft(values[0::2]), small_dft(values[1::2])
    odd = [times_root(v, k, count) for k, v in enumerate(odd)]
    return [add(e, o) for e, o in zip(even, odd)] + [sub(e, o) for e, o in zip(even, odd)]


def long_dft(load, keep, points):
    first = min(8, points)
    second = points // first
    for s in range(second):
        for k, value in enumerate(small_dft([load(e * second + s) for e in range(first)])):
            keep[k * second + s, 0], keep[k * second + s, 1] = times_root(value, s * k, points)
    for k in range(first):
        group = [(keep[k * second + s, 0], keep[k * second + s, 1]) for s in range(second)]
        for j, value in enumerate(small_dft(group)):
            yield k + first * j, value


def split_store(ref, row, rows, re, im):
    for place, part in enumerate((re, im)):
        high = part.astype(jnp.bfloat16)
        low = (part - high.astype(jnp.float32)).astype(jnp.bfloat16)
        ref[0, pl.ds(row, rows), place * LANES : (place + 1) * LANES] = high
        ref[1, pl.ds(row, rows), place * LANES : (place + 1) * LANES] = low


def dot(left, right):
    return jnp.dot(left, right, preferred_element_type=jnp.float32)


def lane_dft(halves, table):
    high, low = halves[0], halves[1]
    return dot(high, table[0]) + dot(low, table[0]) + dot(high, table[1])


def times_twist(twist, k, value):
    re, im = value
    cos, sin = twist[0, pl.ds(k, 1), :], twist[1, pl.ds(k, 1), :]
    return re * cos - im * sin, re * sin + im * cos


def device(me, count, turn, core):
    chips = count // 2
    return 2 * lax.rem(lax.div(me, 2) + turn % chips, chips) + (lax.rem(me, 2) ^ core)


def pack_kernel(units, alone, mirror, lesser, greater, mine, give, *refs):
    *single, places, held, wanted, sems, block_sems = refs
    _, count, tiles, sub, local_len = lesser.shape
    rows = tiles * sub
    me = lax.axis_index("en")
    loads = [pltpu.make_async_copy(mirror, places, sems.at[0])]
    loads += [pltpu.make_async_copy(greater.at[p], held.at[p], sems.at[1 + p]) for p in range(2)]
    offers = [(mine.at[i], *unit, 0) for i, unit in enumerate(units)]
    offers += [(give.at[i], *unit, 1) for i, unit in enumerate(units)]
    offers += [(ref, *one) for ref, one in zip(single, alone)]
    blocks = [
        pltpu.make_async_copy(
            lesser.at[:, device(me, count, turn, core), chunk], ref, block_sems.at[i]
        )
        for i, (ref, chunk, (half, turn), core) in enumerate(offers)
        if not half
    ]
    for copy in loads + blocks:
        copy.start()
    loads[0].wait()
    lane = lax.broadcasted_iota(jnp.int32, (rows, count * rows), 1)
    line = lax.broadcasted_iota(jnp.int32, (rows, count * rows), 0)
    goal = jnp.broadcast_to(places[...], (rows, count * rows)) % rows
    source = jnp.where(goal == line, (lane % rows).astype(jnp.float32), 0.0)
    for to in range(count):
        share = jnp.where(lane // rows == to, source, 0.0)
        order = jnp.sum(share, axis=1, keepdims=True).astype(jnp.int32)
        wanted[to] = jnp.broadcast_to(order, (rows, LANES))
    targets = {}
    for ref, chunk, (half, turn), core in offers:
        if half:
            targets.setdefault((turn, core), {})[chunk] = ref
    for part in range(2):
        loads[1 + part].wait()
        for (turn, core), refs_of in targets.items():
            to = device(me, count, turn, core)
            order = wanted[to]
            for start in range(0, local_len, LANES):
                span = slice(start, start + LANES)
                tiles_in = [held[part, to, u, :, span] for u in range(tiles)]
                for t, ref in refs_of.items():
                    want = order[t * sub : (t + 1) * sub]
                    moved = jnp.zeros((sub, LANES), jnp.float32)
                    for u, tile in enumerate(tiles_in):
                        picked = jnp.take_along_axis(tile, want % sub, axis=0)
                        moved = jnp.where(want // sub == u, picked, moved)
                    ref[part, :, span] = moved
    for copy in blocks:
        copy.wait()


def join_kernel(groups, *refs):
    outs = refs[-len(groups) :]
    for group, out in zip(groups, outs):
        for i, (which, index) in enumerate(group):
            out[2 * i] = refs[2 * which][index]
            out[2 * i + 1] = refs[2 * which + 1][index]


def correlate(got, forward, backward, twist, out, keep, halves, left, right):
    count = got.shape[0] // 2
    rows = got.shape[2]
    steps = got.shape[3] // LANES
    points = count * steps
    own = lax.axis_index("half")

    def read(start, swap):
        def load(t):
            where = slice(t % steps * LANES, (t % steps + 1) * LANES)
            re = got[start + t // steps, 0, :, where]
            im = got[start + t // steps, 1, :, where]
            return (im, re) if swap else (re, im)

        return load

    for which, target in enumerate((left, right)):
        start = jnp.where(own == which, 0, count)
        for k, value in long_dft(read(start, which == 1), keep, points):
            split_store(halves, k * rows, rows, *times_twist(twist, k, value))
        target[...] = lane_dft(halves, forward)

    for k in range(points):
        span = pl.ds(k * rows, rows)
        a_re, a_im = left[span, :LANES], left[span, LANES:]
        b_im, b_re = right[span, :LANES], right[span, LANES:]
        split_store(halves, k * rows, rows, a_re * b_im + a_im * b_re, a_re * b_re - a_im * b_im)
    left[...] = lane_dft(halves, backward)

    def spectrum(k):
        span = pl.ds(k * rows, rows)
        return times_twist(twist, k, (left[span, :LANES], left[span, LANES:]))

    for t, (c_im, c_re) in long_dft(spectrum, keep, points):
        where = slice(t % steps * LANES, (t % steps + 1) * LANES)
        out[t // steps, 0, :, where] = c_im
        out[t // steps, 1, :, where] = -c_re


def pieces_of(refs, held):
    for ref, blocks in zip(refs, held):
        for i, block in enumerate(blocks):
            yield (ref.at[i] if len(blocks) > 1 else ref), *block


def correlate_kernel(chunk, held, bundled, direct, *refs):
    pieces, (forward, backward, twist) = refs[: len(held)], refs[len(held) : len(held) + 3]
    mine, give, *rest = refs[len(held) + 3 :]
    far, (got, out, *scratch) = rest[: 2 * len(direct)], rest[2 * len(direct) :]
    count = out.shape[0]
    own = lax.axis_index("half")
    me = lax.axis_index("en")
    for ref, of, (half, turn), core in pieces_of(pieces, held):
        if of == chunk:
            side = 1 - own if half else own
            got[side * count + device(me, count, -turn, core)] = ref[...]
    correlate(got, forward, backward, twist, out, *scratch)
    for i, turn in enumerate(bundled):
        mine[i] = out[device(me, count, turn, 0)]
        give[i] = out[device(me, count, turn, 1)]
    for i, ref in enumerate(far):
        ref[...] = out[device(me, count, direct[i // 2], i % 2)]


def keep_kernel(held, *refs):
    out, sems = refs[-2:]
    count = out.shape[1]
    me = lax.axis_index("en")
    copies = [
        pltpu.make_async_copy(ref, out.at[:, device(me, count, -turn, core), chunk], sems.at[i])
        for i, (ref, chunk, turn, core) in enumerate(pieces_of(refs, held))
    ]
    for copy in copies:
        copy.start()
    for copy in copies:
        copy.wait()


def call(kernel, out_shape, in_specs, out_specs, scratch=(), mib=4, **settings):
    return pl.pallas_call(
        kernel,
        out_shape=out_shape,
        in_specs=in_specs,
        out_specs=out_specs,
        scratch_shapes=scratch,
        compiler_params=pltpu.CompilerParams(vmem_limit_bytes=mib << 20),
        **settings,
    )


FIRST_ORDER = ((0, 2), (1, 2), (0, 3), (0, 1), (1, 3), (1, 1))


def ordered(values, order):
    return [v for v in order if v in values] + [v for v in values if v not in order]


def plan(chips):
    turns = sorted(range(1, chips), key=lambda turn: (-min(turn, chips - turn), turn))
    arrive = [(half, turn) for turn in turns for half in (1, 0)]
    return ordered(arrive, FIRST_ORDER), [(1, 0), (0, 0)], list(range(1, chips)), [0]


def body(lesser, greater, mirror):
    _, group_rows, local_len = lesser.shape
    count = lax.axis_size("en")
    chips = count // 2
    rows = group_rows // count
    tiles = rows // SUBLANES
    length = local_len * count
    points = length // LANES
    f32 = jnp.float32
    block = jax.ShapeDtypeStruct((2, SUBLANES, local_len), f32)
    tiled = jax.ShapeDtypeStruct((2, count, tiles, SUBLANES, local_len), f32)
    in_vmem = pl.BlockSpec(memory_space=pltpu.VMEM)
    in_hbm = pl.BlockSpec(memory_space=pltpu.HBM)
    dma = pltpu.SemaphoreType.DMA
    far, near, far_back, near_back = plan(chips)

    def stack(pieces):
        return jax.ShapeDtypeStruct((pieces, *block.shape), f32)

    def vmem(shape):
        return pltpu.VMEM(shape.shape, shape.dtype)

    def swap(give):
        return lax.ppermute(give, "en", [(e, e ^ 1) for e in range(count)])

    def join(pairs, groups):
        shapes = [stack(2 * len(group)) for group in groups]
        return call(
            functools.partial(join_kernel, groups),
            shapes,
            [in_vmem] * 2 * len(pairs),
            [in_vmem] * len(groups),
        )(*sum(pairs, ()))

    def send(value, half, turn, core=0):
        if not half + turn + core:
            return value
        pairs = [(h, z, c) for h in range(2) for z in range(chips) for c in range(2)]
        route = [
            (h * count + 2 * z + c, (h ^ half) * count + 2 * ((z + turn) % chips) + (c ^ core))
            for h, z, c in pairs
        ]
        return lax.ppermute(value, ("half", "en"), route)

    mirror, lesser, greater = (
        pltpu.with_memory_space_constraint(x, pltpu.HBM)
        for x in (mirror[None], lesser.reshape(tiled.shape), greater.reshape(tiled.shape))
    )
    tables = (
        jnp.asarray(dft_block(1.0)),
        jnp.asarray(dft_block(length**-1.5)),
        jnp.asarray(twiddles(points)),
    )

    last = tiles - 1
    chunks = range(tiles)
    alone = [(0, t, core) for t in far[:1] for core in range(2)]
    groups = [[(0, t)] for t in far[1:]]
    groups += [[(chunk, t) for chunk in chunks] for t in near]
    groups += [[(chunk, t)] for chunk in chunks[1:] for t in far]
    units = sum(groups, [])
    mine, give, *single = call(
        functools.partial(pack_kernel, units, alone),
        [stack(len(units))] * 2 + [block] * len(alone),
        [in_hbm] * 3,
        [in_vmem] * (2 + len(alone)),
        [
            pltpu.VMEM((1, group_rows), jnp.int32),
            vmem(tiled),
            pltpu.VMEM((count, rows, LANES), jnp.int32),
            dma((3,)),
            dma((2 * len(units) + len(alone),)),
        ],
        mib=8,
    )(mirror, lesser, greater)
    given = swap(give)
    arrived = [send(value, *t, core) for value, (_, t, core) in zip(single, alone)]
    held = [(one,) for one in alone]
    places = iter(range(len(units)))
    joined = join([(mine, given)], [[(0, next(places)) for _ in group] for group in groups])
    for value, group in zip(joined, groups):
        chunk, t = group[0]
        arrived.append(send(value, *t))
        held.append(tuple((*unit, core) for unit in group for core in range(2)))

    kept, pairs, out = [], [], []
    for chunk in chunks:
        direct = far_back[:1] if chunk == last else []
        bundled = far_back[len(direct) :] + near_back
        used = [i for i, blocks in enumerate(held) if any(b[0] == chunk for b in blocks)]
        mine, give, *single = call(
            functools.partial(
                correlate_kernel, chunk, tuple(held[i] for i in used), bundled, direct
            ),
            [stack(len(bundled))] * 2 + [block] * 2 * len(direct),
            [in_vmem] * (len(used) + 3),
            [in_vmem] * (2 + 2 * len(direct)),
            [
                vmem(stack(2 * count)),
                vmem(stack(count)),
                pltpu.VMEM((points, 2, SUBLANES, LANES), f32),
                pltpu.VMEM((2, points * SUBLANES, 2 * LANES), jnp.bfloat16),
                pltpu.VMEM((points * SUBLANES, 2 * LANES), f32),
                pltpu.VMEM((points * SUBLANES, 2 * LANES), f32),
            ],
            mib=16,
            cost_estimate=pl.CostEstimate(
                flops=3 * 2 * 3 * points * SUBLANES * 4 * LANES * LANES,
                bytes_accessed=4 << 20,
                transcendentals=0,
            ),
        )(*(arrived[i] for i in used), *tables)
        returned = [
            (
                send(value, 0, direct[i // 2], i % 2),
                ((chunk, direct[i // 2], i % 2),),
            )
            for i, value in enumerate(single)
        ]
        pairs.append((mine, swap(give)))
        kept.append(bundled)
        groups = [[(chunk, z)] for z in far_back[len(direct) :]]
        if chunk == last:
            groups += [[(c, z) for c in chunks] for z in near_back]
        joined = join(
            pairs if chunk == last else pairs[-1:],
            [[(c if chunk == last else 0, kept[c].index(z)) for c, z in group] for group in groups],
        )
        for value, group in zip(joined, groups):
            z = group[0][1]
            blocks = tuple((*unit, core) for unit in group for core in range(2))
            returned.append((send(value, 0, z), blocks))
        values, blocks = zip(*returned)
        out = [
            call(
                functools.partial(keep_kernel, blocks),
                tiled,
                [in_vmem] * len(values) + [in_hbm] * len(out),
                in_hbm,
                [dma((sum(map(len, blocks)),))],
                mib=1,
                input_output_aliases={len(values): 0} if out else {},
            )(*values, *out)
        ]
    return out[0].reshape(2, group_rows, local_len)


def solution(mesh):
    groups = mesh.shape["grp"]
    devices = mesh.devices.reshape(2, groups // 2, mesh.shape["en"])
    finer = Mesh(devices, ("half", "grp", "en"))
    spec = P(None, ("half", "grp"), "en")
    in_specs = (spec, spec, P(("half", "grp")))

    return jax.shard_map(body, mesh=finer, in_specs=in_specs, out_specs=spec, check_vma=False)
```

```python
import functools
import math

import jax
import jax.numpy as jnp
import numpy as np
from jax import lax
from jax.experimental import pallas as pl
from jax.experimental.pallas import tpu as pltpu
from jax.sharding import Mesh
from jax.sharding import PartitionSpec as P

LANES = 128
SUBLANES = 8


def dft_block(scale):
    turn = 2.0 * math.pi / LANES * (np.outer(np.arange(LANES), np.arange(LANES)) % LANES)
    cos, sin = np.cos(turn), np.sin(turn)
    full = (np.block([[cos, -sin], [sin, cos]]) * scale).astype(np.float32)
    high = full.astype(jnp.bfloat16)
    low = (full - high.astype(np.float32)).astype(jnp.bfloat16)
    return np.stack([high, low])


def twiddles(points):
    length = points * LANES
    turn = 2.0 * math.pi / length * (np.outer(np.arange(points), np.arange(LANES)) % length)
    return np.stack([np.cos(turn), -np.sin(turn)]).astype(np.float32)


def times_root(value, numerator, denominator):
    re, im = value
    eighths = 8 * numerator / denominator % 8
    if eighths == 0:
        return re, im
    if eighths == 2:
        return im, -re
    if eighths == 4:
        return -re, -im
    if eighths == 6:
        return -im, re
    half = math.sqrt(0.5)
    if eighths == 1:
        return (re + im) * half, (im - re) * half
    if eighths == 3:
        return (im - re) * half, -(re + im) * half
    turn = 2.0 * math.pi * numerator / denominator
    cos, sin = math.cos(turn), math.sin(turn)
    return re * cos + im * sin, im * cos - re * sin


def add(a, b):
    return a[0] + b[0], a[1] + b[1]


def sub(a, b):
    return a[0] - b[0], a[1] - b[1]


def small_dft(values):
    count = len(values)
    if count == 1:
        return values
    even, odd = small_dft(values[0::2]), small_dft(values[1::2])
    odd = [times_root(v, k, count) for k, v in enumerate(odd)]
    return [add(e, o) for e, o in zip(even, odd)] + [sub(e, o) for e, o in zip(even, odd)]


def long_dft(load, keep, points):
    first = min(8, points)
    second = points // first
    for s in range(second):
        for k, value in enumerate(small_dft([load(e * second + s) for e in range(first)])):
            keep[k * second + s, 0], keep[k * second + s, 1] = times_root(value, s * k, points)
    for k in range(first):
        group = [(keep[k * second + s, 0], keep[k * second + s, 1]) for s in range(second)]
        for j, value in enumerate(small_dft(group)):
            yield k + first * j, value


def split_store(ref, row, rows, re, im):
    for place, part in enumerate((re, im)):
        high = part.astype(jnp.bfloat16)
        low = (part - high.astype(jnp.float32)).astype(jnp.bfloat16)
        ref[0, pl.ds(row, rows), place * LANES : (place + 1) * LANES] = high
        ref[1, pl.ds(row, rows), place * LANES : (place + 1) * LANES] = low


def dot(left, right):
    return jnp.dot(left, right, preferred_element_type=jnp.float32)


def lane_dft(halves, table):
    high, low = halves[0], halves[1]
    return dot(high, table[0]) + dot(low, table[0]) + dot(high, table[1])


def times_twist(twist, k, value):
    re, im = value
    cos, sin = twist[0, pl.ds(k, 1), :], twist[1, pl.ds(k, 1), :]
    return re * cos - im * sin, re * sin + im * cos


def device(me, count, turn, core):
    chips = count // 2
    return 2 * lax.rem(lax.div(me, 2) + turn % chips, chips) + (lax.rem(me, 2) ^ core)


def pack_kernel(units, alone, mirror, lesser, greater, mine, give, *refs):
    *single, places, held, wanted, sems, block_sems = refs
    _, count, tiles, sub, local_len = lesser.shape
    rows = tiles * sub
    me = lax.axis_index("en")
    loads = [pltpu.make_async_copy(mirror, places, sems.at[0])]
    loads += [pltpu.make_async_copy(greater.at[p], held.at[p], sems.at[1 + p]) for p in range(2)]
    offers = [(mine.at[i], *unit, 0) for i, unit in enumerate(units)]
    offers += [(give.at[i], *unit, 1) for i, unit in enumerate(units)]
    offers += [(ref, *one) for ref, one in zip(single, alone)]
    blocks = [
        pltpu.make_async_copy(
            lesser.at[:, device(me, count, turn, core), chunk], ref, block_sems.at[i]
        )
        for i, (ref, chunk, (half, turn), core) in enumerate(offers)
        if not half
    ]
    for copy in loads + blocks:
        copy.start()
    loads[0].wait()
    lane = lax.broadcasted_iota(jnp.int32, (rows, count * rows), 1)
    line = lax.broadcasted_iota(jnp.int32, (rows, count * rows), 0)
    goal = jnp.broadcast_to(places[...], (rows, count * rows)) % rows
    source = jnp.where(goal == line, (lane % rows).astype(jnp.float32), 0.0)
    for to in range(count):
        share = jnp.where(lane // rows == to, source, 0.0)
        order = jnp.sum(share, axis=1, keepdims=True).astype(jnp.int32)
        wanted[to] = jnp.broadcast_to(order, (rows, LANES))
    targets = {}
    for ref, chunk, (half, turn), core in offers:
        if half:
            targets.setdefault((turn, core), {})[chunk] = ref
    for part in range(2):
        loads[1 + part].wait()
        for (turn, core), refs_of in targets.items():
            to = device(me, count, turn, core)
            order = wanted[to]
            for start in range(0, local_len, LANES):
                span = slice(start, start + LANES)
                tiles_in = [held[part, to, u, :, span] for u in range(tiles)]
                for t, ref in refs_of.items():
                    want = order[t * sub : (t + 1) * sub]
                    moved = jnp.zeros((sub, LANES), jnp.float32)
                    for u, tile in enumerate(tiles_in):
                        picked = jnp.take_along_axis(tile, want % sub, axis=0)
                        moved = jnp.where(want // sub == u, picked, moved)
                    ref[part, :, span] = moved
    for copy in blocks:
        copy.wait()


def join_kernel(groups, *refs):
    outs = refs[-len(groups) :]
    for group, out in zip(groups, outs):
        for i, (which, index) in enumerate(group):
            out[2 * i] = refs[2 * which][index]
            out[2 * i + 1] = refs[2 * which + 1][index]


def correlate(got, forward, backward, twist, out, keep, halves, left, right):
    count = got.shape[0] // 2
    rows = got.shape[2]
    steps = got.shape[3] // LANES
    points = count * steps
    own = lax.axis_index("half")

    def read(start, swap):
        def load(t):
            where = slice(t % steps * LANES, (t % steps + 1) * LANES)
            re = got[start + t // steps, 0, :, where]
            im = got[start + t // steps, 1, :, where]
            return (im, re) if swap else (re, im)

        return load

    for which, target in enumerate((left, right)):
        start = jnp.where(own == which, 0, count)
        for k, value in long_dft(read(start, which == 1), keep, points):
            split_store(halves, k * rows, rows, *times_twist(twist, k, value))
        target[...] = lane_dft(halves, forward)

    for k in range(points):
        span = pl.ds(k * rows, rows)
        a_re, a_im = left[span, :LANES], left[span, LANES:]
        b_im, b_re = right[span, :LANES], right[span, LANES:]
        split_store(halves, k * rows, rows, a_re * b_im + a_im * b_re, a_re * b_re - a_im * b_im)
    left[...] = lane_dft(halves, backward)

    def spectrum(k):
        span = pl.ds(k * rows, rows)
        return times_twist(twist, k, (left[span, :LANES], left[span, LANES:]))

    for t, (c_im, c_re) in long_dft(spectrum, keep, points):
        where = slice(t % steps * LANES, (t % steps + 1) * LANES)
        out[t // steps, 0, :, where] = c_im
        out[t // steps, 1, :, where] = -c_re


def pieces_of(refs, held):
    for ref, blocks in zip(refs, held):
        for i, block in enumerate(blocks):
            yield (ref.at[i] if len(blocks) > 1 else ref), *block


def correlate_kernel(chunk, held, bundled, direct, *refs):
    pieces, (forward, backward, twist) = refs[: len(held)], refs[len(held) : len(held) + 3]
    mine, give, *rest = refs[len(held) + 3 :]
    far, (got, out, *scratch) = rest[: 2 * len(direct)], rest[2 * len(direct) :]
    count = out.shape[0]
    own = lax.axis_index("half")
    me = lax.axis_index("en")
    for ref, of, (half, turn), core in pieces_of(pieces, held):
        if of == chunk:
            side = 1 - own if half else own
            got[side * count + device(me, count, -turn, core)] = ref[...]
    correlate(got, forward, backward, twist, out, *scratch)
    for i, turn in enumerate(bundled):
        mine[i] = out[device(me, count, turn, 0)]
        give[i] = out[device(me, count, turn, 1)]
    for i, ref in enumerate(far):
        ref[...] = out[device(me, count, direct[i // 2], i % 2)]


def keep_kernel(held, *refs):
    out, sems = refs[-2:]
    count = out.shape[1]
    me = lax.axis_index("en")
    copies = [
        pltpu.make_async_copy(ref, out.at[:, device(me, count, -turn, core), chunk], sems.at[i])
        for i, (ref, chunk, turn, core) in enumerate(pieces_of(refs, held))
    ]
    for copy in copies:
        copy.start()
    for copy in copies:
        copy.wait()


def call(kernel, out_shape, in_specs, out_specs, scratch=(), mib=4, **settings):
    return pl.pallas_call(
        kernel,
        out_shape=out_shape,
        in_specs=in_specs,
        out_specs=out_specs,
        scratch_shapes=scratch,
        compiler_params=pltpu.CompilerParams(vmem_limit_bytes=mib << 20),
        **settings,
    )


FIRST_ORDER = ((0, 2), (1, 2), (0, 3), (0, 1), (1, 3), (1, 1))


def ordered(values, order):
    return [v for v in order if v in values] + [v for v in values if v not in order]


def plan(chips):
    turns = sorted(range(1, chips), key=lambda turn: (-min(turn, chips - turn), turn))
    arrive = [(half, turn) for turn in turns for half in (1, 0)]
    return ordered(arrive, FIRST_ORDER), [(1, 0), (0, 0)], list(range(1, chips)), [0]


def body(lesser, greater, mirror):
    _, group_rows, local_len = lesser.shape
    count = lax.axis_size("en")
    chips = count // 2
    rows = group_rows // count
    tiles = rows // SUBLANES
    length = local_len * count
    points = length // LANES
    f32 = jnp.float32
    block = jax.ShapeDtypeStruct((2, SUBLANES, local_len), f32)
    tiled = jax.ShapeDtypeStruct((2, count, tiles, SUBLANES, local_len), f32)
    in_vmem = pl.BlockSpec(memory_space=pltpu.VMEM)
    in_hbm = pl.BlockSpec(memory_space=pltpu.HBM)
    dma = pltpu.SemaphoreType.DMA
    far, near, far_back, near_back = plan(chips)

    def stack(pieces):
        return jax.ShapeDtypeStruct((pieces, *block.shape), f32)

    def vmem(shape):
        return pltpu.VMEM(shape.shape, shape.dtype)

    def swap(give):
        return lax.ppermute(give, "en", [(e, e ^ 1) for e in range(count)])

    def join(pairs, groups):
        shapes = [stack(2 * len(group)) for group in groups]
        return call(
            functools.partial(join_kernel, groups),
            shapes,
            [in_vmem] * 2 * len(pairs),
            [in_vmem] * len(groups),
        )(*sum(pairs, ()))

    def send(value, half, turn, core=0):
        if not half + turn + core:
            return value
        pairs = [(h, z, c) for h in range(2) for z in range(chips) for c in range(2)]
        route = [
            (h * count + 2 * z + c, (h ^ half) * count + 2 * ((z + turn) % chips) + (c ^ core))
            for h, z, c in pairs
        ]
        return lax.ppermute(value, ("half", "en"), route)

    mirror, lesser, greater = (
        pltpu.with_memory_space_constraint(x, pltpu.HBM)
        for x in (mirror[None], lesser.reshape(tiled.shape), greater.reshape(tiled.shape))
    )
    tables = (
        jnp.asarray(dft_block(1.0)),
        jnp.asarray(dft_block(length**-1.5)),
        jnp.asarray(twiddles(points)),
    )

    last = tiles - 1
    chunks = range(tiles)
    alone = [(0, t, core) for t in far[:1] for core in range(2)]
    groups = [[(0, t)] for t in far[1:]]
    groups += [[(chunk, t) for chunk in chunks] for t in near]
    groups += [[(chunk, t)] for chunk in chunks[1:] for t in far]
    units = sum(groups, [])
    mine, give, *single = call(
        functools.partial(pack_kernel, units, alone),
        [stack(len(units))] * 2 + [block] * len(alone),
        [in_hbm] * 3,
        [in_vmem] * (2 + len(alone)),
        [
            pltpu.VMEM((1, group_rows), jnp.int32),
            vmem(tiled),
            pltpu.VMEM((count, rows, LANES), jnp.int32),
            dma((3,)),
            dma((2 * len(units) + len(alone),)),
        ],
        mib=8,
    )(mirror, lesser, greater)
    given = swap(give)
    arrived = [send(value, *t, core) for value, (_, t, core) in zip(single, alone)]
    held = [(one,) for one in alone]
    places = iter(range(len(units)))
    joined = join([(mine, given)], [[(0, next(places)) for _ in group] for group in groups])
    for value, group in zip(joined, groups):
        chunk, t = group[0]
        arrived.append(send(value, *t))
        held.append(tuple((*unit, core) for unit in group for core in range(2)))

    kept, pairs, keeps, out = [], [], [], []
    for chunk in chunks:
        direct = far_back[:1] if chunk == last else []
        bundled = far_back[len(direct) :] + near_back
        used = [i for i, blocks in enumerate(held) if any(b[0] == chunk for b in blocks)]
        mine, give, *single = call(
            functools.partial(
                correlate_kernel, chunk, tuple(held[i] for i in used), bundled, direct
            ),
            [stack(len(bundled))] * 2 + [block] * 2 * len(direct),
            [in_vmem] * (len(used) + 3),
            [in_vmem] * (2 + 2 * len(direct)),
            [
                vmem(stack(2 * count)),
                vmem(stack(count)),
                pltpu.VMEM((points, 2, SUBLANES, LANES), f32),
                pltpu.VMEM((2, points * SUBLANES, 2 * LANES), jnp.bfloat16),
                pltpu.VMEM((points * SUBLANES, 2 * LANES), f32),
                pltpu.VMEM((points * SUBLANES, 2 * LANES), f32),
            ],
            mib=16,
            cost_estimate=pl.CostEstimate(
                flops=3 * 2 * 3 * points * SUBLANES * 4 * LANES * LANES,
                bytes_accessed=4 << 20,
                transcendentals=0,
            ),
        )(*(arrived[i] for i in used), *tables)
        returned = [
            (
                send(value, 0, direct[i // 2], i % 2),
                ((chunk, direct[i // 2], i % 2),),
            )
            for i, value in enumerate(single)
        ]
        pairs.append((mine, swap(give)))
        kept.append(bundled)
        groups = [[(chunk, z)] for z in far_back[len(direct) :]]
        if chunk == last:
            groups += [[(c, z) for c in chunks] for z in near_back]
        joined = join(
            pairs if chunk == last else pairs[-1:],
            [[(c if chunk == last else 0, kept[c].index(z)) for c, z in group] for group in groups],
        )
        for value, group in zip(joined, groups):
            z = group[0][1]
            blocks = tuple((*unit, core) for unit in group for core in range(2))
            returned.append((send(value, 0, z), blocks))
        stays = [one for one in returned if one[1][0][1] == 0]
        leaves = [one for one in returned if one[1][0][1] != 0]
        keeps.append(leaves)
        keeps[0] += stays
    for chunk, returned in enumerate(keeps):
        values, blocks = zip(*returned)
        out = [
            call(
                functools.partial(keep_kernel, blocks),
                tiled,
                [in_vmem] * len(values) + [in_hbm] * len(out),
                in_hbm,
                [dma((sum(map(len, blocks)),))],
                mib=1,
                input_output_aliases={len(values): 0} if out else {},
            )(*values, *out)
        ]
    return out[0].reshape(2, group_rows, local_len)


def solution(mesh):
    groups = mesh.shape["grp"]
    devices = mesh.devices.reshape(2, groups // 2, mesh.shape["en"])
    finer = Mesh(devices, ("half", "grp", "en"))
    spec = P(None, ("half", "grp"), "en")
    in_specs = (spec, spec, P(("half", "grp")))

    return jax.shard_map(body, mesh=finer, in_specs=in_specs, out_specs=spec, check_vma=False)
```

```python
import functools
import math

import jax
import jax.numpy as jnp
import numpy as np
from jax import lax
from jax.experimental import pallas as pl
from jax.experimental.pallas import tpu as pltpu
from jax.sharding import Mesh
from jax.sharding import PartitionSpec as P

LANES = 128
SUBLANES = 8


def dft_block(scale):
    turn = 2.0 * math.pi / LANES * (np.outer(np.arange(LANES), np.arange(LANES)) % LANES)
    cos, sin = np.cos(turn), np.sin(turn)
    full = (np.block([[cos, -sin], [sin, cos]]) * scale).astype(np.float32)
    high = full.astype(jnp.bfloat16)
    low = (full - high.astype(np.float32)).astype(jnp.bfloat16)
    return np.stack([high, low])


def twiddles(points):
    length = points * LANES
    turn = 2.0 * math.pi / length * (np.outer(np.arange(points), np.arange(LANES)) % length)
    return np.stack([np.cos(turn), -np.sin(turn)]).astype(np.float32)


def times_root(value, numerator, denominator):
    re, im = value
    eighths = 8 * numerator / denominator % 8
    if eighths == 0:
        return re, im
    if eighths == 2:
        return im, -re
    if eighths == 4:
        return -re, -im
    if eighths == 6:
        return -im, re
    half = math.sqrt(0.5)
    if eighths == 1:
        return (re + im) * half, (im - re) * half
    if eighths == 3:
        return (im - re) * half, -(re + im) * half
    turn = 2.0 * math.pi * numerator / denominator
    cos, sin = math.cos(turn), math.sin(turn)
    return re * cos + im * sin, im * cos - re * sin


def add(a, b):
    return a[0] + b[0], a[1] + b[1]


def sub(a, b):
    return a[0] - b[0], a[1] - b[1]


def small_dft(values):
    count = len(values)
    if count == 1:
        return values
    even, odd = small_dft(values[0::2]), small_dft(values[1::2])
    odd = [times_root(v, k, count) for k, v in enumerate(odd)]
    return [add(e, o) for e, o in zip(even, odd)] + [sub(e, o) for e, o in zip(even, odd)]


def long_dft(load, keep, points):
    first = min(8, points)
    second = points // first
    for s in range(second):
        for k, value in enumerate(small_dft([load(e * second + s) for e in range(first)])):
            keep[k * second + s, 0], keep[k * second + s, 1] = times_root(value, s * k, points)
    for k in range(first):
        group = [(keep[k * second + s, 0], keep[k * second + s, 1]) for s in range(second)]
        for j, value in enumerate(small_dft(group)):
            yield k + first * j, value


def split_store(ref, row, rows, re, im):
    for place, part in enumerate((re, im)):
        high = part.astype(jnp.bfloat16)
        low = (part - high.astype(jnp.float32)).astype(jnp.bfloat16)
        ref[0, pl.ds(row, rows), place * LANES : (place + 1) * LANES] = high
        ref[1, pl.ds(row, rows), place * LANES : (place + 1) * LANES] = low


def dot(left, right):
    return jnp.dot(left, right, preferred_element_type=jnp.float32)


def lane_dft(halves, table):
    high, low = halves[0], halves[1]
    return dot(high, table[0]) + dot(low, table[0]) + dot(high, table[1])


def times_twist(twist, k, value):
    re, im = value
    cos, sin = twist[0, pl.ds(k, 1), :], twist[1, pl.ds(k, 1), :]
    return re * cos - im * sin, re * sin + im * cos


def device(me, count, turn, core):
    chips = count // 2
    return 2 * lax.rem(lax.div(me, 2) + turn % chips, chips) + (lax.rem(me, 2) ^ core)


def pack_kernel(units, alone, mirror, lesser, greater, mine, give, *refs):
    *single, places, held, wanted, sems, block_sems = refs
    _, count, tiles, sub, local_len = lesser.shape
    rows = tiles * sub
    me = lax.axis_index("en")
    loads = [pltpu.make_async_copy(mirror, places, sems.at[0])]
    loads += [pltpu.make_async_copy(greater.at[p], held.at[p], sems.at[1 + p]) for p in range(2)]
    offers = [(mine.at[i], *unit, 0) for i, unit in enumerate(units)]
    offers += [(give.at[i], *unit, 1) for i, unit in enumerate(units)]
    offers += [(ref, *one) for ref, one in zip(single, alone)]
    blocks = [
        pltpu.make_async_copy(
            lesser.at[:, device(me, count, turn, core), chunk], ref, block_sems.at[i]
        )
        for i, (ref, chunk, (half, turn), core) in enumerate(offers)
        if not half
    ]
    for copy in loads + blocks:
        copy.start()
    loads[0].wait()
    lane = lax.broadcasted_iota(jnp.int32, (rows, count * rows), 1)
    line = lax.broadcasted_iota(jnp.int32, (rows, count * rows), 0)
    goal = jnp.broadcast_to(places[...], (rows, count * rows)) % rows
    source = jnp.where(goal == line, (lane % rows).astype(jnp.float32), 0.0)
    for to in range(count):
        share = jnp.where(lane // rows == to, source, 0.0)
        order = jnp.sum(share, axis=1, keepdims=True).astype(jnp.int32)
        wanted[to] = jnp.broadcast_to(order, (rows, LANES))
    targets = {}
    for ref, chunk, (half, turn), core in offers:
        if half:
            targets.setdefault((turn, core), {})[chunk] = ref
    for part in range(2):
        loads[1 + part].wait()
        for (turn, core), refs_of in targets.items():
            to = device(me, count, turn, core)
            order = wanted[to]
            for start in range(0, local_len, LANES):
                span = slice(start, start + LANES)
                tiles_in = [held[part, to, u, :, span] for u in range(tiles)]
                for t, ref in refs_of.items():
                    want = order[t * sub : (t + 1) * sub]
                    moved = jnp.zeros((sub, LANES), jnp.float32)
                    for u, tile in enumerate(tiles_in):
                        picked = jnp.take_along_axis(tile, want % sub, axis=0)
                        moved = jnp.where(want // sub == u, picked, moved)
                    ref[part, :, span] = moved
    for copy in blocks:
        copy.wait()


def join_kernel(groups, *refs):
    outs = refs[-len(groups) :]
    for group, out in zip(groups, outs):
        for i, (which, index) in enumerate(group):
            out[2 * i] = refs[2 * which][index]
            out[2 * i + 1] = refs[2 * which + 1][index]


def correlate(got, forward, backward, twist, out, keep, halves, left, right):
    count = got.shape[0] // 2
    rows = got.shape[2]
    steps = got.shape[3] // LANES
    points = count * steps
    own = lax.axis_index("half")

    def read(start, swap):
        def load(t):
            where = slice(t % steps * LANES, (t % steps + 1) * LANES)
            re = got[start + t // steps, 0, :, where]
            im = got[start + t // steps, 1, :, where]
            return (im, re) if swap else (re, im)

        return load

    for which, target in enumerate((left, right)):
        start = jnp.where(own == which, 0, count)
        for k, value in long_dft(read(start, which == 1), keep, points):
            split_store(halves, k * rows, rows, *times_twist(twist, k, value))
        target[...] = lane_dft(halves, forward)

    for k in range(points):
        span = pl.ds(k * rows, rows)
        a_re, a_im = left[span, :LANES], left[span, LANES:]
        b_im, b_re = right[span, :LANES], right[span, LANES:]
        split_store(halves, k * rows, rows, a_re * b_im + a_im * b_re, a_re * b_re - a_im * b_im)
    left[...] = lane_dft(halves, backward)

    def spectrum(k):
        span = pl.ds(k * rows, rows)
        return times_twist(twist, k, (left[span, :LANES], left[span, LANES:]))

    for t, (c_im, c_re) in long_dft(spectrum, keep, points):
        where = slice(t % steps * LANES, (t % steps + 1) * LANES)
        out[t // steps, 0, :, where] = c_im
        out[t // steps, 1, :, where] = -c_re


def pieces_of(refs, held):
    for ref, blocks in zip(refs, held):
        for i, block in enumerate(blocks):
            yield (ref.at[i] if len(blocks) > 1 else ref), *block


def correlate_kernel(chunk, held, bundled, direct, *refs):
    pieces, (forward, backward, twist) = refs[: len(held)], refs[len(held) : len(held) + 3]
    mine, give, *rest = refs[len(held) + 3 :]
    far, (got, out, *scratch) = rest[: 2 * len(direct)], rest[2 * len(direct) :]
    count = out.shape[0]
    own = lax.axis_index("half")
    me = lax.axis_index("en")
    for ref, of, (half, turn), core in pieces_of(pieces, held):
        if of == chunk:
            side = 1 - own if half else own
            got[side * count + device(me, count, -turn, core)] = ref[...]
    correlate(got, forward, backward, twist, out, *scratch)
    for i, turn in enumerate(bundled):
        mine[i] = out[device(me, count, turn, 0)]
        give[i] = out[device(me, count, turn, 1)]
    for i, ref in enumerate(far):
        ref[...] = out[device(me, count, direct[i // 2], i % 2)]


def keep_kernel(held, *refs):
    out, sems = refs[-2:]
    count = out.shape[1]
    me = lax.axis_index("en")
    copies = [
        pltpu.make_async_copy(ref, out.at[:, device(me, count, -turn, core), chunk], sems.at[i])
        for i, (ref, chunk, turn, core) in enumerate(pieces_of(refs, held))
    ]
    for copy in copies:
        copy.start()
    for copy in copies:
        copy.wait()


def call(kernel, out_shape, in_specs, out_specs, scratch=(), mib=4, **settings):
    return pl.pallas_call(
        kernel,
        out_shape=out_shape,
        in_specs=in_specs,
        out_specs=out_specs,
        scratch_shapes=scratch,
        compiler_params=pltpu.CompilerParams(vmem_limit_bytes=mib << 20),
        **settings,
    )


FIRST_ORDER = ((0, 2), (1, 2), (0, 3), (0, 1), (1, 3), (1, 1))


def ordered(values, order):
    return [v for v in order if v in values] + [v for v in values if v not in order]


def plan(chips):
    turns = sorted(range(1, chips), key=lambda turn: (-min(turn, chips - turn), turn))
    arrive = [(half, turn) for turn in turns for half in (1, 0)]
    return ordered(arrive, FIRST_ORDER), [(1, 0), (0, 0)], list(range(1, chips)), [0]


def body(lesser, greater, mirror):
    _, group_rows, local_len = lesser.shape
    count = lax.axis_size("en")
    chips = count // 2
    rows = group_rows // count
    tiles = rows // SUBLANES
    length = local_len * count
    points = length // LANES
    f32 = jnp.float32
    block = jax.ShapeDtypeStruct((2, SUBLANES, local_len), f32)
    tiled = jax.ShapeDtypeStruct((2, count, tiles, SUBLANES, local_len), f32)
    in_vmem = pl.BlockSpec(memory_space=pltpu.VMEM)
    in_hbm = pl.BlockSpec(memory_space=pltpu.HBM)
    dma = pltpu.SemaphoreType.DMA
    far, near, far_back, near_back = plan(chips)

    def stack(pieces):
        return jax.ShapeDtypeStruct((pieces, *block.shape), f32)

    def vmem(shape):
        return pltpu.VMEM(shape.shape, shape.dtype)

    def swap(give):
        return lax.ppermute(give, "en", [(e, e ^ 1) for e in range(count)])

    def join(pairs, groups):
        shapes = [stack(2 * len(group)) for group in groups]
        return call(
            functools.partial(join_kernel, groups),
            shapes,
            [in_vmem] * 2 * len(pairs),
            [in_vmem] * len(groups),
        )(*sum(pairs, ()))

    def send(value, half, turn, core=0):
        if not half + turn + core:
            return value
        pairs = [(h, z, c) for h in range(2) for z in range(chips) for c in range(2)]
        route = [
            (h * count + 2 * z + c, (h ^ half) * count + 2 * ((z + turn) % chips) + (c ^ core))
            for h, z, c in pairs
        ]
        return lax.ppermute(value, ("half", "en"), route)

    mirror, lesser, greater = (
        pltpu.with_memory_space_constraint(x, pltpu.HBM)
        for x in (mirror[None], lesser.reshape(tiled.shape), greater.reshape(tiled.shape))
    )
    tables = (
        jnp.asarray(dft_block(1.0)),
        jnp.asarray(dft_block(length**-1.5)),
        jnp.asarray(twiddles(points)),
    )

    last = tiles - 1
    chunks = range(tiles)
    alone = [(0, t, core) for t in far[:1] for core in range(2)]
    groups = [[(0, t)] for t in far[1:]]
    groups += [[(chunk, t) for chunk in chunks] for t in near]
    groups += [[(chunk, t)] for chunk in chunks[1:] for t in far]
    units = sum(groups, [])
    mine, give, *single = call(
        functools.partial(pack_kernel, units, alone),
        [stack(len(units))] * 2 + [block] * len(alone),
        [in_hbm] * 3,
        [in_vmem] * (2 + len(alone)),
        [
            pltpu.VMEM((1, group_rows), jnp.int32),
            vmem(tiled),
            pltpu.VMEM((count, rows, LANES), jnp.int32),
            dma((3,)),
            dma((2 * len(units) + len(alone),)),
        ],
        mib=8,
    )(mirror, lesser, greater)
    given = swap(give)
    arrived = [send(value, *t, core) for value, (_, t, core) in zip(single, alone)]
    held = [(one,) for one in alone]
    places = iter(range(len(units)))
    joined = join([(mine, given)], [[(0, next(places)) for _ in group] for group in groups])
    for value, group in zip(joined, groups):
        chunk, t = group[0]
        arrived.append(send(value, *t))
        held.append(tuple((*unit, core) for unit in group for core in range(2)))

    kept, pairs, keeps, out = [], [], [], []
    for chunk in chunks:
        direct = far_back[:1] if chunk == last else []
        bundled = far_back[len(direct) :] + near_back
        used = [i for i, blocks in enumerate(held) if any(b[0] == chunk for b in blocks)]
        mine, give, *single = call(
            functools.partial(
                correlate_kernel, chunk, tuple(held[i] for i in used), bundled, direct
            ),
            [stack(len(bundled))] * 2 + [block] * 2 * len(direct),
            [in_vmem] * (len(used) + 3),
            [in_vmem] * (2 + 2 * len(direct)),
            [
                vmem(stack(2 * count)),
                vmem(stack(count)),
                pltpu.VMEM((points, 2, SUBLANES, LANES), f32),
                pltpu.VMEM((2, points * SUBLANES, 2 * LANES), jnp.bfloat16),
                pltpu.VMEM((points * SUBLANES, 2 * LANES), f32),
                pltpu.VMEM((points * SUBLANES, 2 * LANES), f32),
            ],
            mib=16,
            cost_estimate=pl.CostEstimate(
                flops=3 * 2 * 3 * points * SUBLANES * 4 * LANES * LANES,
                bytes_accessed=4 << 20,
                transcendentals=0,
            ),
        )(*(arrived[i] for i in used), *tables)
        returned = [
            (
                send(value, 0, direct[i // 2], i % 2),
                ((chunk, direct[i // 2], i % 2),),
            )
            for i, value in enumerate(single)
        ]
        pairs.append((mine, swap(give)))
        kept.append(bundled)
        groups = [[(chunk, z)] for z in far_back[len(direct) :]]
        if chunk == last:
            groups += [[(c, z) for c in chunks] for z in near_back]
        joined = join(
            pairs if chunk == last else pairs[-1:],
            [[(c if chunk == last else 0, kept[c].index(z)) for c, z in group] for group in groups],
        )
        for value, group in zip(joined, groups):
            z = group[0][1]
            blocks = tuple((*unit, core) for unit in group for core in range(2))
            returned.append((send(value, 0, z), blocks))
        soon = [len(held_by) == 1 or held_by[0][1] == 0 for _, held_by in returned]
        keeps.append([one for one, early in zip(returned, soon) if not early])
        keeps[0] += [one for one, early in zip(returned, soon) if early]
    for chunk, returned in enumerate(keeps):
        values, blocks = zip(*returned)
        out = [
            call(
                functools.partial(keep_kernel, blocks),
                tiled,
                [in_vmem] * len(values) + [in_hbm] * len(out),
                in_hbm,
                [dma((sum(map(len, blocks)),))],
                mib=1,
                input_output_aliases={len(values): 0} if out else {},
            )(*values, *out)
        ]
    return out[0].reshape(2, group_rows, local_len)


def solution(mesh):
    groups = mesh.shape["grp"]
    devices = mesh.devices.reshape(2, groups // 2, mesh.shape["en"])
    finer = Mesh(devices, ("half", "grp", "en"))
    spec = P(None, ("half", "grp"), "en")
    in_specs = (spec, spec, P(("half", "grp")))

    return jax.shard_map(body, mesh=finer, in_specs=in_specs, out_specs=spec, check_vma=False)
```
